512 devices in a mesh: scene: 128 (over y, z, core), view: 4 (over x).
Axes of the slice: x: 4, y: 8, z: 8, core: 2. Of those that a mesh axis runs over, the one named last changes fastest.
Arguments:
- features: bfloat16 [4096, 64, 128], P('scene'), may hold values from -6 to 6
- means: float32 [4096, 3, 128], P('scene'), may hold values from -5 to 5
- conics: float32 [4096, 3, 128], P('scene'), may hold values from -0.12 to 0.3, as said below
- opacity: float32 [4096, 128], P('scene'), may hold values from -6 to -3
- camera: float32 [4, 2, 4], P('view'), may hold values from -6 to 6
- lists: int32 [4, 1024, 4], P('view', 'scene'), may hold values from 0 to 4095, as said below
- masks: int32 [4, 1024, 512], P('view', 'scene'), may hold values 0 or 1
- cotangent: bfloat16 [4, 1024, 64, 256], P('view', 'scene'), may hold values from -6 to 6
Outputs:
- grad_features: float32 [4096, 64, 128], P('scene', 'view')
- grad_means: float32 [4096, 3, 128], P('scene')
- grad_conics: float32 [4096, 3, 128], P('scene')
- grad_opacity: float32 [4096, 128], P('scene')
The draws below stay inside these ranges and needn't reach their ends.
Inputs may be any that keep to these rules, and one draw needn't show every extreme that they name: `lists`: an id names block id % 32 of owner id // 32. The 4 ids of one tile are distinct. Among the 8 tiles of one device (one view, one index of scene), at most 1 distinct block belongs to one owner and at most 2 entries name blocks of one owner; both bounds are reached on every device. `conics`: a and c are positive and b * b < a * c for every Gaussian.
All inputs are finite; a program needn't handle non-finite values. No bound on the sum of `masks` on one device may be relied on, other than what follows from the above.
Results may differ from the reference program's by a relative error of at most 0.0055.
Values may be sent and summed in bfloat16 or wider, within the bound.
No kernel may reach another device: no remote copies, remote signals or barrier semaphores. Data moves between devices by JAX's collectives and lax.ppermute only.
A program may use at most 64 MiB of HBM per device.

```python
import math
import jax
import jax.numpy as jnp
from jax import lax

F = 64
BLK = 128
NB = 4
PIX = 256
TILES_DEV = 8
BLOCKS_DEV = 32
VIEWS = 4
TILES = 1024
BLOCKS = 4096
UNIQ = 28
REP = 4
CAP = 1
N_SCENE = 128


def draw_conics(key, part):
    key_a, key_c, key_b = jax.random.split(key, 3)
    coef_a = jnp.exp(jax.random.uniform(key_a, (BLOCKS, BLK), jnp.float32, jnp.log(0.03), jnp.log(0.3)))
    coef_c = jnp.exp(jax.random.uniform(key_c, (BLOCKS, BLK), jnp.float32, jnp.log(0.03), jnp.log(0.3)))
    coef_b = jax.random.uniform(key_b, (BLOCKS, BLK), jnp.float32, -0.4, 0.4) * jnp.sqrt(coef_a * coef_c)
    return jnp.stack([coef_a, coef_b, coef_c], axis=1).astype(jnp.float32)


def draw_lists(key, part):
    device_keys = jax.random.split(key, VIEWS * N_SCENE)

    def draw_device(device_key):
        key_owner, key_block, key_tile = jax.random.split(device_key, 3)
        owners = jax.random.permutation(key_owner, N_SCENE).astype(jnp.int32)
        block_keys = jax.random.split(key_block, N_SCENE)
        block_perm = jax.vmap(lambda sub_key: jax.random.permutation(sub_key, BLOCKS_DEV))(block_keys).astype(jnp.int32)
        pool = jnp.arange(UNIQ, dtype=jnp.int32)
        owner_slot = pool % N_SCENE
        depth = pool // N_SCENE
        pool_ids = owners[owner_slot] * BLOCKS_DEV + block_perm[owner_slot, depth]
        repeats = jnp.arange(REP, dtype=jnp.int32)
        picked = repeats % CAP * N_SCENE + repeats // CAP
        entries = jnp.concatenate([pool_ids, pool_ids[picked]]).reshape(TILES_DEV, NB)
        tile_order = jax.random.permutation(key_tile, TILES_DEV)
        return entries[tile_order]
    drawn = jax.vmap(draw_device)(device_keys)
    return drawn.reshape(VIEWS, N_SCENE * TILES_DEV, NB).astype(jnp.int32)


def set_ends(values, rng, low, top_value):
    extent = values.shape
    index_at = [jax.random.randint(jax.random.fold_in(rng, axis), (), 0, extent[axis]) for axis in range(len(extent))]
    values = values.at[tuple(index_at)].set(low)
    longest = extent.index(max(extent))
    index_at[longest] = (index_at[longest] + 1) % extent[longest]
    return values.at[tuple(index_at)].set(top_value)


def block_levels(key, extent, pieces, least, largest):
    level, own = 1.0, jax.random.fold_in(key, 6)
    for axis_at, parts in pieces:
        steps = jnp.exp(jax.random.uniform(jax.random.fold_in(own, axis_at), (parts,), jnp.float32, least / len(pieces), largest / len(pieces)))
        level = level * jnp.repeat(steps, extent[axis_at] // parts).reshape([-1 if axis == axis_at else 1 for axis in range(len(extent))])
    return level


def normal_values(own_key, dims, width, most, shards=(), kind=jnp.bfloat16):
    loudness = block_levels(own_key, dims, shards, -0.22, 0.18) if shards else 1.0
    array = jax.random.normal(own_key, dims, jnp.float32) * width * loudness
    return jnp.minimum(jnp.maximum(array, -most), most).astype(kind)


def setup_inputs(seed: int = 0) -> dict:
    key_of = jax.random.split(jax.random.key(seed), 9)
    features = normal_values(key_of[0], (BLOCKS, F, BLK), 1.0, 6.0, ((0, 128),))
    means = normal_values(key_of[1], (BLOCKS, 3, BLK), 1.0, 5.0, ((0, 128),), jnp.float32)
    conics = draw_conics(jax.random.fold_in(key_of[8], 71), 0)
    opacity = jnp.clip(-6.0 + 3.0 * jax.random.uniform(key_of[3], (BLOCKS, BLK), jnp.float32) ** block_levels(key_of[3], (BLOCKS, BLK), ((0, 128),), -0.2, 0.2), -6.0, -3.0)
    camera = normal_values(key_of[4], (VIEWS, 2, 4), 2.0, 6.0, ((0, 4),), jnp.float32)
    lists = draw_lists(jax.random.fold_in(key_of[8], 71), 0)
    masks = set_ends((jax.random.randint(key_of[6], (VIEWS, TILES, NB * BLK), 0, 4) < 3).astype(jnp.int32), jax.random.fold_in(key_of[6], 1), 0, 1)
    cotangent = normal_values(key_of[7], (VIEWS, TILES, F, PIX), 1.0, 6.0, ((0, 4), (1, 128)))
    return {"features": features, "means": means, "conics": conics, "opacity": opacity, "camera": camera, "lists": lists, "masks": masks, "cotangent": cotangent}


def blend_weights(means, conics, opacity, mask, camera, pixels):
    row_count = opacity.shape[0] * opacity.shape[1]
    tile_side = math.isqrt(pixels)
    screen_x = camera[0, 0] * means[:, 0] + camera[0, 1] * means[:, 1] + camera[0, 2] * means[:, 2] + camera[0, 3]
    screen_y = camera[1, 0] * means[:, 0] + camera[1, 1] * means[:, 1] + camera[1, 2] * means[:, 2] + camera[1, 3]
    pixel_ids = jnp.arange(pixels, dtype=jnp.int32)
    coord_u = (pixel_ids % tile_side).astype(jnp.float32) - 0.5 * (tile_side - 1)
    coord_w = (pixel_ids // tile_side).astype(jnp.float32) - 0.5 * (tile_side - 1)
    delta_x = coord_u[:, None] - screen_x.reshape(1, row_count)
    delta_y = coord_w[:, None] - screen_y.reshape(1, row_count)
    quadratic = conics[:, 0].reshape(1, row_count) * delta_x * delta_x + 2.0 * conics[:, 1].reshape(1, row_count) * delta_x * delta_y + conics[:, 2].reshape(1, row_count) * delta_y * delta_y
    alphas = mask.astype(jnp.float32)[None, :] * jax.nn.sigmoid(opacity.reshape(1, row_count)) * jnp.exp(-0.5 * quadratic)
    log_keep = jnp.log1p(-alphas)
    transmit = jnp.exp(jnp.cumsum(log_keep, axis=1) - log_keep)
    return (transmit * alphas).astype(jnp.bfloat16)

def tile_grads(feats, means, conics, opacity, mask, camera, cotangent):
    per_tile, channels, block_rows = feats.shape
    pixels = cotangent.shape[1]
    feat_rows = jnp.transpose(feats, (1, 0, 2)).reshape(channels, per_tile * block_rows)
    cot_float = cotangent.astype(jnp.float32)

    def geometry_loss(means, conics, opacity):
        weight = blend_weights(means, conics, opacity, mask, camera, pixels)
        color = lax.dot_general(feat_rows, weight, (((1,), (1,)), ((), ())), preferred_element_type=jnp.float32)
        return (jnp.sum(cot_float * color), weight)
    geo_grads, weight = jax.grad(geometry_loss, argnums=(0, 1, 2), has_aux=True)(means, conics, opacity)
    grad_rows = lax.dot_general(cotangent, weight, (((1,), (0,)), ((), ())), preferred_element_type=jnp.float32)
    grad_feats = jnp.transpose(grad_rows.reshape(channels, per_tile, block_rows), (1, 0, 2))
    return (grad_feats, geo_grads[0], geo_grads[1], geo_grads[2])

def reference(features, means, conics, opacity, camera, lists, masks, cotangent):
    totals = (jnp.zeros((BLOCKS, F, BLK), jnp.float32), jnp.zeros((BLOCKS, 3, BLK), jnp.float32), jnp.zeros((BLOCKS, 3, BLK), jnp.float32), jnp.zeros((BLOCKS, BLK), jnp.float32))
    for view_index in range(VIEWS):
        view_camera = camera[view_index]

        def scan_step(totals, inputs):
            block_ids, mask_group, cot_group = inputs
            tile_out = jax.vmap(tile_grads, in_axes=(0, 0, 0, 0, 0, None, 0))(features[block_ids], means[block_ids], conics[block_ids], opacity[block_ids], mask_group, view_camera, cot_group)
            flat_ids = block_ids.reshape(-1)
            new_totals = tuple((total_arr.at[flat_ids].add(tile_arr.reshape((flat_ids.shape[0],) + tile_arr.shape[2:])) for total_arr, tile_arr in zip(totals, tile_out)))
            return (new_totals, None)
        inputs = (lists[view_index].reshape(N_SCENE, TILES_DEV, NB), masks[view_index].reshape(N_SCENE, TILES_DEV, NB * BLK), cotangent[view_index].reshape(N_SCENE, TILES_DEV, F, PIX))
        totals, _ = lax.scan(scan_step, totals, inputs)
    return (totals[0], totals[1], totals[2], totals[3])
```

```python
import math

import jax
import jax.numpy as jnp
from jax import lax
from jax.experimental import pallas as pl
from jax.experimental.pallas import tpu as pltpu
from jax.sharding import PartitionSpec as P

VMEM = pltpu.MemorySpace.VMEM
SMEM = pltpu.MemorySpace.SMEM
LOG2E = math.log2(math.e)
GEO = 8


def call(kernel, outs, n_smem, n_vmem, scratch=(), name=None):
    return pl.pallas_call(
        kernel,
        out_shape=outs,
        in_specs=[pl.BlockSpec(memory_space=SMEM)] * n_smem
        + [pl.BlockSpec(memory_space=VMEM)] * n_vmem,
        out_specs=[pl.BlockSpec(memory_space=VMEM)] * len(outs),
        scratch_shapes=scratch,
        compiler_params=pltpu.CompilerParams(vmem_limit_bytes=56 * 1024 * 1024),
        name=name,
    )


def table_kernel(cam, feats, means, conics, opac, table):
    channels = feats.shape[1]
    bf16, f32 = jnp.bfloat16, jnp.float32

    def step(i, carry):
        m = means[i]
        screen = [
            cam[k, 0] * m[0:1] + cam[k, 1] * m[1:2] + cam[k, 2] * m[2:3] + cam[k, 3]
            for k in (0, 1)
        ]
        q = conics[i]
        rows = screen + [q[0:1], q[1:2], q[2:3], opac[pl.ds(i, 1), :]]
        full = stack_rows(rows)
        hi = full.astype(bf16).astype(f32)
        rest = full - hi
        mid = rest.astype(bf16).astype(f32)
        low = rest - mid
        first = stack_rows([hi[k : k + 1] for k in range(6)] + [low[2:3], low[3:4]])
        second = stack_rows([mid[k : k + 1] for k in range(6)] + [low[4:5]])
        geo = jnp.concatenate([first, second], axis=0).astype(bf16)
        table[i] = jnp.concatenate([feats[i], geo], axis=0)
        return carry

    lax.fori_loop(0, feats.shape[0], step, 0, unroll=4)


def answer_kernel(req, table, out):
    def step(i, carry):
        out[i] = table[jnp.maximum(req[i], 0)]
        return carry

    lax.fori_loop(0, out.shape[0], step, 0, unroll=8)


def split_bf16(x):
    hi = x.astype(jnp.bfloat16)
    return hi, (x - hi.astype(jnp.float32)).astype(jnp.bfloat16)


def stack_rows(rows):
    n = rows[0].shape[1]
    row_id = lax.broadcasted_iota(jnp.int32, (GEO, n), 0)
    out = jnp.zeros((GEO, n), jnp.float32)
    for i, row in enumerate(rows):
        out = jnp.where(row_id == i, jnp.broadcast_to(row, (GEO, n)), out)
    return out


def tile_kernel(
    slot, first, cam, fetched, masks, cots, out,
    acc, ebuf, abuf, lhi, llo, wbuf, tri, ones, quad, quad_t,
):
    tiles, channels, pixels = cots.shape
    side = math.isqrt(pixels)
    per_tile = slot.shape[0] // tiles
    blk = fetched.shape[2]
    rows = per_tile * blk
    half = rows // 2
    f32, bf16 = jnp.float32, jnp.bfloat16

    ki = lax.broadcasted_iota(jnp.int32, (half, half), 0)
    ri = lax.broadcasted_iota(jnp.int32, (half, half), 1)
    tri[0] = jnp.where(ki < ri, 1.0, 0.0).astype(bf16)
    tri[1] = jnp.where(ki > ri, 1.0, 0.0).astype(bf16)
    ones[...] = jnp.ones((half, half), bf16)

    def monomials(shape, pix_dim):
        pix = lax.broadcasted_iota(jnp.int32, shape, pix_dim)
        col = lax.broadcasted_iota(jnp.int32, shape, 1 - pix_dim) % GEO
        u = (pix % side).astype(f32) - 0.5 * (side - 1)
        w = (pix // side).astype(f32) - 0.5 * (side - 1)
        val = jnp.where(col == 0, 1.0, 0.0)
        for i, m in enumerate((u, w, u * u, u * w, w * w)):
            val = jnp.where(col == i + 1, m, val)
        return val.astype(bf16)

    quad[...] = monomials(quad.shape, 0)
    quad_t[...] = monomials(quad_t.shape, 1)

    def dot(a, b):
        return jnp.dot(a, b, preferred_element_type=f32)

    def one_tile(t, carry):
        entry = [t * per_tile + j for j in range(per_tile)]
        slots = [slot[e] for e in entry]
        parts = jnp.concatenate([fetched[s, channels:] for s in slots], axis=1).astype(f32)
        g = parts[:GEO] + parts[GEO:]
        sx, sy, op = g[0:1], g[1:2], g[5:6]
        a = g[2:3] + parts[6:7]
        b = g[3:4] + parts[7:8]
        c = g[4:5] + parts[14:15]
        live = masks[pl.ds(t, 1), :]
        ax_by = a * sx + b * sy
        bx_cy = b * sx + c * sy
        neg = jnp.exp(-op)
        log_sig = -jnp.log(1.0 + neg)
        one_less = neg / (1.0 + neg)
        const = log_sig - 0.5 * (sx * ax_by + sy * bx_cy)
        const = jnp.where(live > 0, const * LOG2E, -1e30)
        coef = stack_rows(
            [
                const,
                ax_by * LOG2E,
                bx_cy * LOG2E,
                a * (-0.5 * LOG2E),
                b * (-LOG2E),
                c * (-0.5 * LOG2E),
            ]
        )
        hi = coef.astype(bf16).astype(f32)
        rest = coef - hi
        mid = rest.astype(bf16).astype(f32)
        coefs = jnp.concatenate([hi, mid, rest - mid, jnp.zeros_like(hi)], axis=0).astype(bf16)

        alpha = jnp.exp2(dot(quad[...], coefs))
        abuf[...] = alpha
        keep = jnp.log(1.0 - alpha)
        k_hi, k_lo = split_bf16(keep)
        lhi[...] = k_hi
        llo[...] = k_lo
        ebuf[...] = jnp.exp(-keep)

        up = tri[0]
        for q in (0, 1):
            cols = slice(q * half, (q + 1) * half)
            pre = dot(lhi[:, cols], up) + dot(llo[:, cols], up)
            if q:
                pre += dot(lhi[:, :half], ones[...]) + dot(llo[:, :half], ones[...])
            weight = jnp.exp(pre) * abuf[:, cols]
            wbuf[:, cols] = weight
        cot = cots[t]
        grad_feats = dot(cot, wbuf[...].astype(bf16))
        feat_rows = jnp.concatenate([fetched[s, :channels] for s in slots], axis=1)
        grad_weight = lax.dot_general(
            cot, feat_rows, (((0,), (0,)), ((), ())), preferred_element_type=f32
        ).astype(bf16).astype(f32)
        flow = wbuf[...] * grad_weight
        wbuf[...] = flow
        f_hi, f_lo = split_bf16(flow)
        lhi[...] = f_hi
        llo[...] = f_lo
        low = tri[1]
        for q in (0, 1):
            cols = slice(q * half, (q + 1) * half)
            behind = dot(lhi[:, cols], low) + dot(llo[:, cols], low)
            if not q:
                behind += dot(lhi[:, half:], ones[...]) + dot(llo[:, half:], ones[...])
            wbuf[:, cols] = wbuf[:, cols] - abuf[:, cols] * ebuf[:, cols] * behind
        g_hi, g_lo = split_bf16(wbuf[...])
        mom = dot(quad_t[...], g_hi) + dot(quad_t[...], g_lo)
        m0, mu, mw, muu, muw, mww = [mom[i : i + 1] for i in range(6)]
        dx = mu - sx * m0
        dy = mw - sy * m0
        dxx = muu - sx * (mu + dx)
        dxy = muw - sx * mw - sy * dx
        dyy = mww - sy * (mw + dy)
        gsx = a * dx + b * dy
        gsy = b * dx + c * dy
        grad_geo = stack_rows(
            [
                cam[0, 0] * gsx + cam[1, 0] * gsy,
                cam[0, 1] * gsx + cam[1, 1] * gsy,
                cam[0, 2] * gsx + cam[1, 2] * gsy,
                -0.5 * dxx,
                -dxy,
                -0.5 * dyy,
                one_less * m0,
            ]
        )
        for j in range(per_tile):
            lanes = slice(j * blk, (j + 1) * blk)
            val = jnp.concatenate([grad_feats[:, lanes], grad_geo[:, lanes]], axis=0)
            at = first[entry[j]]
            acc[at] = jnp.where(at == entry[j], val, acc[at] + val)
        return carry

    lax.fori_loop(0, tiles, one_tile, 0)

    def give(e, carry):
        out[slot[e]] = acc[first[e]].astype(bf16)
        return carry

    lax.fori_loop(0, slot.shape[0], give, 0, unroll=4)


def owner_kernel(req, view, got, own, *rest):
    sends, acc = rest[:-1], rest[-1]
    views = len(sends) + 1
    blocks, out_rows, _ = own.shape
    share = out_rows - GEO
    acc[...] = jnp.zeros_like(acc)

    def step(i, carry):
        at = req[i]

        @pl.when(at >= 0)
        def _():
            acc[at] = acc[at] + got[i].astype(jnp.float32)

        return carry

    lax.fori_loop(0, got.shape[0], step, 0, unroll=4)

    def lay(i, carry):
        geo = acc[i, views * share :]
        for d, ref in enumerate((own,) + sends):
            start = pl.multiple_of(lax.rem(view[0] + d, views) * share, share)
            rows = jnp.concatenate([acc[i, pl.ds(start, share)], geo], axis=0)
            ref[i] = rows.astype(ref.dtype)
        return carry

    lax.fori_loop(0, blocks, lay, 0, unroll=2)


def view_kernel(own, *rest):
    got, (out_feats, out_means, out_conics, out_opac) = rest[:-4], rest[-4:]
    share = out_feats.shape[1]
    total = own[...]
    for ref in got:
        total = total + ref[...].astype(jnp.float32)
    out_feats[...] = total[:, :share]
    geo = total[:, share:]
    out_means[...] = geo[:, 0:3]
    out_conics[...] = geo[:, 3:6]
    out_opac[...] = geo[:, 6]


def run_tiles(owner, first, cam, fetched, masks, cots):
    n_scene, _, blk = fetched.shape
    channels = cots.shape[1]
    entries = owner.shape[0]
    tiles, _, pixels = cots.shape
    rows = entries // tiles * blk
    f32, bf16 = jnp.float32, jnp.bfloat16
    return call(
        tile_kernel,
        [jax.ShapeDtypeStruct((n_scene, channels + GEO, blk), bf16)],
        3, 3,
        scratch=[
            pltpu.VMEM((entries, channels + GEO, blk), f32),
            pltpu.VMEM((pixels, rows), f32),
            pltpu.VMEM((pixels, rows), f32),
            pltpu.VMEM((pixels, rows), bf16),
            pltpu.VMEM((pixels, rows), bf16),
            pltpu.VMEM((pixels, rows), f32),
            pltpu.VMEM((2, rows // 2, rows // 2), bf16),
            pltpu.VMEM((rows // 2, rows // 2), bf16),
            pltpu.VMEM((pixels, 4 * GEO), bf16),
            pltpu.VMEM((2 * GEO, pixels), bf16),
        ],
        name="tiles",
    )(owner, first, cam, fetched, masks, cots)[0]


def body(features, means, conics, opacity, camera, lists, masks, cotangent):
    n_scene = lax.axis_size("scene")
    n_view = lax.axis_size("view")
    blocks_dev, channels, blk = features.shape
    tiles_dev, per_tile = lists.shape[1:]
    f32, bf16, i32 = jnp.float32, jnp.bfloat16, jnp.int32
    cam = camera[0]

    ids = lists[0].reshape(-1)
    entries = ids.shape[0]
    owner = ids // blocks_dev
    local = ids % blocks_dev
    wanted = jnp.max(
        jnp.where(owner[:, None] == jnp.arange(n_scene, dtype=i32)[None, :], local[:, None], -1),
        axis=0,
    )
    position = jnp.arange(entries, dtype=i32)
    first = jnp.min(
        jnp.where(owner[:, None] == owner[None, :], position[None, :], entries), axis=1
    )
    req = lax.all_to_all(wanted, "scene", split_axis=0, concat_axis=0, tiled=True)

    width = channels + 2 * GEO
    (table,) = call(
        table_kernel, [jax.ShapeDtypeStruct((blocks_dev, width, blk), bf16)], 1, 4, name="table"
    )(cam, features, means, conics, opacity)
    (answers,) = call(
        answer_kernel, [jax.ShapeDtypeStruct((n_scene, width, blk), bf16)], 1, 1, name="answer"
    )(req, table)
    fetched = lax.all_to_all(answers, "scene", split_axis=0, concat_axis=0, tiled=True)
    grads_out = run_tiles(owner, first, cam, fetched, masks[0], cotangent[0])
    grads_in = lax.all_to_all(grads_out, "scene", split_axis=0, concat_axis=0, tiled=True)

    share = channels // n_view
    piece = (blocks_dev, share + GEO, blk)
    own, *sends = call(
        owner_kernel,
        [jax.ShapeDtypeStruct(piece, f32)]
        + [jax.ShapeDtypeStruct(piece, bf16)] * (n_view - 1),
        2, 1,
        scratch=[pltpu.VMEM((blocks_dev, channels + GEO, blk), f32)],
        name="owner",
    )(req, lax.axis_index("view").reshape(1), grads_in)
    got = [
        lax.ppermute(send, "view", [(v, (v + d) % n_view) for v in range(n_view)])
        for d, send in enumerate(sends, 1)
    ]
    return tuple(
        call(
            view_kernel,
            [
                jax.ShapeDtypeStruct((blocks_dev, share, blk), f32),
                jax.ShapeDtypeStruct((blocks_dev, 3, blk), f32),
                jax.ShapeDtypeStruct((blocks_dev, 3, blk), f32),
                jax.ShapeDtypeStruct((blocks_dev, blk), f32),
            ],
            0, n_view, name="views",
        )(own, *got)
    )


def solution(mesh):
    return jax.shard_map(
        body,
        mesh=mesh,
        in_specs=(
            P("scene", None, None),
            P("scene", None, None),
            P("scene", None, None),
            P("scene", None),
            P("view", None, None),
            P("view", "scene", None),
            P("view", "scene", None),
            P("view", "scene", None, None),
        ),
        out_specs=(
            P("scene", "view", None),
            P("scene", None, None),
            P("scene", None, None),
            P("scene", None),
        ),
        check_vma=False,
    )
```

```python
import math

import jax
import jax.numpy as jnp
from jax import lax
from jax.experimental import pallas as pl
from jax.experimental.pallas import tpu as pltpu
from jax.sharding import PartitionSpec as P

VMEM = pltpu.MemorySpace.VMEM
SMEM = pltpu.MemorySpace.SMEM
GEO = 8
ABREAST = 2


def call(kernel, outs, n_smem, n_vmem, scratch=(), name=None, mib=8):
    return pl.pallas_call(
        kernel,
        out_shape=outs,
        in_specs=[pl.BlockSpec(memory_space=SMEM)] * n_smem
        + [pl.BlockSpec(memory_space=VMEM)] * n_vmem,
        out_specs=[pl.BlockSpec(memory_space=VMEM)] * len(outs),
        scratch_shapes=scratch,
        compiler_params=pltpu.CompilerParams(vmem_limit_bytes=mib * 1024 * 1024),
        name=name,
    )


def want_kernel(blocks_dev, ids, want):
    want[...] = jnp.full(want.shape, -1, jnp.int32)
    for j in range(ids.shape[0]):
        for t in range(ids.shape[1]):
            owner = lax.div(ids[j, t], blocks_dev)
            want[owner] = jnp.full((1, want.shape[2]), ids[j, t] - owner * blocks_dev, jnp.int32)


def stack_rows(rows):
    n = rows[0].shape[1]
    row_id = lax.broadcasted_iota(jnp.int32, (GEO, n), 0)
    out = jnp.zeros((GEO, n), jnp.float32)
    for i, row in enumerate(rows):
        out = jnp.where(row_id == i, jnp.broadcast_to(row, (GEO, n)), out)
    return out


def table_kernel(cam, feats, means, conics, opac, table):
    bf16, f32 = jnp.bfloat16, jnp.float32

    def step(i, carry):
        at = pl.ds(i, 1)
        m = [means[k, at, :] for k in range(3)]
        screen = [
            cam[k, 0] * m[0] + cam[k, 1] * m[1] + cam[k, 2] * m[2] + cam[k, 3] for k in (0, 1)
        ]
        full = stack_rows(screen + [conics[k, at, :] for k in range(3)] + [opac[at, :]])
        hi = full.astype(bf16).astype(f32)
        rest = full - hi
        mid = rest.astype(bf16).astype(f32)
        low = rest - mid
        first = stack_rows([hi[k : k + 1] for k in range(6)] + [low[2:3], low[3:4]])
        second = stack_rows([mid[k : k + 1] for k in range(6)] + [low[4:5]])
        geo = jnp.concatenate([first, second], axis=0).astype(bf16)
        table[i] = jnp.concatenate([feats[i], geo], axis=0)
        return carry

    lax.fori_loop(0, feats.shape[0], step, 0, unroll=4)


def answer_kernel(view, asked, table, out, req, req_smem, sem):
    n = asked.shape[0]
    lane = lax.broadcasted_iota(jnp.int32, (1, n), 1)
    line = jnp.full((1, n), -1, jnp.int32)
    for i in range(n):
        line = jnp.where(lane == i, asked[i], line)
    req[0] = line
    req[1] = jnp.full((1, n), view[0], jnp.int32)
    copy = pltpu.make_async_copy(req.at[0], req_smem, sem)
    copy.start()
    copy.wait()

    def step(i, carry):
        out[i] = table[jnp.maximum(req_smem[0, i], 0)]
        return carry

    lax.fori_loop(0, n, step, 0, unroll=8)


def tile_kernel(
    blocks_dev, ids, cam, fetched, masks, cots, out,
    acc, abuf, ebuf, keeps, weights, flows, prefix, suffix, quad, quad_t, seen,
):
    tiles, channels, pixels = cots.shape
    side = math.isqrt(pixels)
    per_tile = ids.shape[0]
    n_scene, _, blk = fetched.shape
    rows = per_tile * blk
    half = rows // 2
    f32, bf16 = jnp.float32, jnp.bfloat16

    def dot(a, b):
        return jnp.dot(a, b, preferred_element_type=f32)

    ki = lax.broadcasted_iota(jnp.int32, (half, half), 0)
    ri = lax.broadcasted_iota(jnp.int32, (half, half), 1)
    one = jnp.ones((half, half), bf16)
    up = jnp.where(ki < ri, 1.0, 0.0).astype(bf16)
    prefix[: 2 * half] = jnp.concatenate([one, one], axis=0)
    prefix[2 * half :] = jnp.concatenate([up, up], axis=0)
    suffix[:half] = jnp.where(ki > ri, 1.0, 0.0).astype(bf16)
    suffix[half:] = one

    def monomials(shape, pix_dim):
        pix = lax.broadcasted_iota(jnp.int32, shape, pix_dim)
        col = lax.broadcasted_iota(jnp.int32, shape, 1 - pix_dim) % GEO
        u = (pix % side).astype(f32) - 0.5 * (side - 1)
        w = (pix // side).astype(f32) - 0.5 * (side - 1)
        val = jnp.where(col == 0, 1.0, 0.0)
        for i, m in enumerate((u, w, u * u, u * w, w * w)):
            val = jnp.where(col == i + 1, m, val)
        return val.astype(bf16)

    quad[...] = monomials(quad.shape, 0)
    quad_t[...] = monomials(quad_t.shape, 1)

    def clear(i, carry):
        seen[i] = -1
        return carry

    lax.fori_loop(0, n_scene, clear, 0, unroll=8)

    def one_tile(t, n):
        slots = [lax.div(ids[j, t], blocks_dev) for j in range(per_tile)]
        parts = jnp.concatenate([fetched[s, channels:] for s in slots], axis=1).astype(f32)
        g = parts[:GEO] + parts[GEO:]
        sx, sy, op = g[0:1], g[1:2], g[5:6]
        a = g[2:3] + parts[6:7]
        b = g[3:4] + parts[7:8]
        c = g[4:5] + parts[14:15]
        live = masks[pl.ds(t, 1), :]
        ax_by = a * sx + b * sy
        bx_cy = b * sx + c * sy
        neg = jnp.exp(-op)
        log_sig = -jnp.log(1.0 + neg)
        one_less = neg / (1.0 + neg)
        const = log_sig - 0.5 * (sx * ax_by + sy * bx_cy)
        const = jnp.where(live > 0, const, -1e30)
        coef = stack_rows(
            [
                const,
                ax_by,
                bx_cy,
                -0.5 * a,
                -b,
                -0.5 * c,
            ]
        )
        hi = coef.astype(bf16).astype(f32)
        rest = coef - hi
        mid = rest.astype(bf16).astype(f32)
        coefs = jnp.concatenate([hi, mid, rest - mid, jnp.zeros_like(hi)], axis=0).astype(bf16)

        for q in (0, 1):
            cols = slice(q * half, (q + 1) * half)
            power = dot(quad[...], coefs[:, cols])
            alpha = jnp.exp(power)
            abuf[n, :, cols] = alpha
            keep = jnp.log(1.0 - alpha)
            keep_hi = keep.astype(bf16)
            keeps[n, :, 2 * q * half : (2 * q + 1) * half] = keep_hi
            keeps[n, :, (2 * q + 1) * half : (2 * q + 2) * half] = (
                keep - keep_hi.astype(f32)
            ).astype(bf16)
            ebuf[n, :, cols] = jnp.exp(power - keep)

        cot = cots[t]
        feat_rows = jnp.concatenate([fetched[s, :channels] for s in slots], axis=1)
        for q in (0, 1):
            cols = slice(q * half, (q + 1) * half)
            if q:
                before = dot(keeps[n], prefix[...])
            else:
                before = dot(keeps[n, :, : 2 * half], prefix[2 * half :])
            weight = jnp.exp(before) * abuf[n, :, cols]
            weights[n, :, cols] = weight.astype(bf16)
            flow = weight * lax.dot_general(
                cot, feat_rows[:, cols], (((0,), (0,)), ((), ())), preferred_element_type=f32
            )
            abuf[n, :, cols] = flow
            flows[n, :, cols] = flow.astype(bf16)
        grad_feats = dot(cot, weights[n])
        for q in (0, 1):
            cols = slice(q * half, (q + 1) * half)
            if q:
                behind = dot(flows[n, :, half:], suffix[:half])
            else:
                behind = dot(flows[n], suffix[...])
            weights[n, :, cols] = (abuf[n, :, cols] - ebuf[n, :, cols] * behind).astype(bf16)
        mom = dot(quad_t[...], weights[n])
        m0, mu, mw, muu, muw, mww = [mom[i : i + 1] for i in range(6)]
        dx = mu - sx * m0
        dy = mw - sy * m0
        dxx = muu - sx * (mu + dx)
        dxy = muw - sx * mw - sy * dx
        dyy = mww - sy * (mw + dy)
        gsx = a * dx + b * dy
        gsy = b * dx + c * dy
        grad_geo = stack_rows(
            [
                cam[0, 0] * gsx + cam[1, 0] * gsy,
                cam[0, 1] * gsx + cam[1, 1] * gsy,
                cam[0, 2] * gsx + cam[1, 2] * gsy,
                -0.5 * dxx,
                -dxy,
                -0.5 * dyy,
                one_less * m0,
            ]
        )
        for j in range(per_tile):
            lanes = slice(j * blk, (j + 1) * blk)
            val = jnp.concatenate([grad_feats[:, lanes], grad_geo[:, lanes]], axis=0)
            mine = t * per_tile + j
            held = seen[slots[j]]
            at = jnp.where(held < 0, mine, held)
            seen[slots[j]] = at
            acc[at] = jnp.where(at == mine, val, acc[at] + val)

    def some_tiles(i, carry):
        for n in range(ABREAST):
            one_tile(i * ABREAST + n, n)
        return carry

    lax.fori_loop(0, tiles // ABREAST, some_tiles, 0)

    def give(t, carry):
        for j in range(per_tile):
            s = lax.div(ids[j, t], blocks_dev)
            out[s] = acc[seen[s]].astype(bf16)
        return carry

    lax.fori_loop(0, tiles, give, 0)


def owner_kernel(req, got, own, *rest):
    sends, acc = rest[:-1], rest[-1]
    views = len(sends) + 1
    blocks, out_rows, _ = own.shape
    share = out_rows - GEO
    acc[...] = jnp.zeros_like(acc)

    def step(i, carry):
        at = req[0, 0, i]

        @pl.when(at >= 0)
        def _():
            acc[at] = acc[at] + got[i].astype(jnp.float32)

        return carry

    lax.fori_loop(0, got.shape[0], step, 0, unroll=4)

    def lay(i, carry):
        geo = acc[i, views * share :]
        for d, ref in enumerate((own,) + sends):
            start = pl.multiple_of(lax.rem(req[1, 0, 0] + d, views) * share, share)
            rows = jnp.concatenate([acc[i, pl.ds(start, share)], geo], axis=0)
            ref[i] = rows.astype(ref.dtype)
        return carry

    lax.fori_loop(0, blocks, lay, 0, unroll=2)


def view_kernel(own, *rest):
    got, (out_feats, out_means, out_conics, out_opac) = rest[:-4], rest[-4:]
    share = out_feats.shape[1]
    total = own[...]
    for ref in got:
        total = total + ref[...].astype(jnp.float32)
    out_feats[...] = total[:, :share]
    geo = total[:, share:]
    for k in range(3):
        out_means[k] = geo[:, k]
        out_conics[k] = geo[:, 3 + k]
    out_opac[...] = geo[:, 6]


def run_tiles(ids, cam, fetched, masks, cots, blocks_dev):
    n_scene, _, blk = fetched.shape
    tiles, channels, pixels = cots.shape
    entries = tiles * ids.shape[0]
    rows = ids.shape[0] * blk
    f32, bf16 = jnp.float32, jnp.bfloat16
    return call(
        lambda *refs: tile_kernel(blocks_dev, *refs),
        [jax.ShapeDtypeStruct((n_scene, channels + GEO, blk), bf16)],
        2, 3,
        scratch=[
            pltpu.VMEM((entries, channels + GEO, blk), f32),
            pltpu.VMEM((ABREAST, pixels, rows), f32),
            pltpu.VMEM((ABREAST, pixels, rows), f32),
            pltpu.VMEM((ABREAST, pixels, 2 * rows), bf16),
            pltpu.VMEM((ABREAST, pixels, rows), bf16),
            pltpu.VMEM((ABREAST, pixels, rows), bf16),
            pltpu.VMEM((2 * rows, rows // 2), bf16),
            pltpu.VMEM((rows, rows // 2), bf16),
            pltpu.VMEM((pixels, 4 * GEO), bf16),
            pltpu.VMEM((2 * GEO, pixels), bf16),
            pltpu.SMEM((n_scene,), jnp.int32),
        ],
        name="tiles",
        mib=24,
    )(ids, cam, fetched, masks, cots)[0]


def body(features, means, conics, opacity, camera, lists, masks, cotangent):
    n_scene = lax.axis_size("scene")
    n_view = lax.axis_size("view")
    blocks_dev, channels, blk = features.shape
    f32, bf16, i32 = jnp.float32, jnp.bfloat16, jnp.int32
    cam = camera[0]
    ids = lists[0].T

    (want,) = call(
        lambda *refs: want_kernel(blocks_dev, *refs),
        [jax.ShapeDtypeStruct((n_scene, 1, n_scene), i32)],
        1, 0, name="want",
    )(ids)
    asked = lax.all_to_all(want, "scene", split_axis=0, concat_axis=0, tiled=True)
    width = channels + 2 * GEO
    (table,) = call(
        table_kernel, [jax.ShapeDtypeStruct((blocks_dev, width, blk), bf16)], 1, 4, name="table"
    )(cam, features, means.transpose(1, 0, 2), conics.transpose(1, 0, 2), opacity)
    answers, req = call(
        answer_kernel,
        [
            jax.ShapeDtypeStruct((n_scene, width, blk), bf16),
            jax.ShapeDtypeStruct((2, 1, n_scene), i32),
        ],
        1, 2,
        scratch=[pltpu.SMEM((1, n_scene), i32), pltpu.SemaphoreType.DMA],
        name="answer",
    )(lax.axis_index("view").reshape(1), asked, table)
    fetched = lax.all_to_all(answers, "scene", split_axis=0, concat_axis=0, tiled=True)
    grads_out = run_tiles(ids, cam, fetched, masks[0], cotangent[0], blocks_dev)
    grads_in = lax.all_to_all(grads_out, "scene", split_axis=0, concat_axis=0, tiled=True)

    share = channels // n_view
    piece = (blocks_dev, share + GEO, blk)
    own, *sends = call(
        owner_kernel,
        [jax.ShapeDtypeStruct(piece, f32)]
        + [jax.ShapeDtypeStruct(piece, bf16)] * (n_view - 1),
        1, 1,
        scratch=[pltpu.VMEM((blocks_dev, channels + GEO, blk), f32)],
        name="owner",
    )(req, grads_in)
    got = [
        lax.ppermute(send, "view", [(v, (v + d) % n_view) for v in range(n_view)])
        for d, send in enumerate(sends, 1)
    ]
    grad_feats, grad_means, grad_conics, grad_opac = call(
        view_kernel,
        [
            jax.ShapeDtypeStruct((blocks_dev, share, blk), f32),
            jax.ShapeDtypeStruct((3, blocks_dev, blk), f32),
            jax.ShapeDtypeStruct((3, blocks_dev, blk), f32),
            jax.ShapeDtypeStruct((blocks_dev, blk), f32),
        ],
        0, n_view, name="views",
    )(own, *got)
    return grad_feats, grad_means.transpose(1, 0, 2), grad_conics.transpose(1, 0, 2), grad_opac


def solution(mesh):
    return jax.shard_map(
        body,
        mesh=mesh,
        in_specs=(
            P("scene", None, None),
            P("scene", None, None),
            P("scene", None, None),
            P("scene", None),
            P("view", None, None),
            P("view", "scene", None),
            P("view", "scene", None),
            P("view", "scene", None, None),
        ),
        out_specs=(
            P("scene", "view", None),
            P("scene", None, None),
            P("scene", None, None),
            P("scene", None),
        ),
        check_vma=False,
    )
```

```python
import math

import jax
import jax.numpy as jnp
from jax import lax
from jax.experimental import pallas as pl
from jax.experimental.pallas import tpu as pltpu
from jax.sharding import PartitionSpec as P

VMEM = pltpu.MemorySpace.VMEM
SMEM = pltpu.MemorySpace.SMEM
GEO = 8
ABREAST = 2


def call(kernel, outs, n_smem, n_vmem, scratch=(), name=None, mib=8):
    return pl.pallas_call(
        kernel,
        out_shape=outs,
        in_specs=[pl.BlockSpec(memory_space=SMEM)] * n_smem
        + [pl.BlockSpec(memory_space=VMEM)] * n_vmem,
        out_specs=[pl.BlockSpec(memory_space=VMEM)] * len(outs),
        scratch_shapes=scratch,
        compiler_params=pltpu.CompilerParams(vmem_limit_bytes=mib * 1024 * 1024),
        name=name,
    )


def want_kernel(blocks_dev, lists, want, ids, sem):
    copy = pltpu.make_async_copy(lists, ids, sem)
    copy.start()
    want[...] = jnp.full(want.shape, -1, jnp.int32)
    copy.wait()
    for j in range(ids.shape[0]):
        for t in range(ids.shape[1]):
            owner = lax.div(ids[j, t], blocks_dev)
            want[owner] = jnp.full((1, want.shape[2]), ids[j, t] - owner * blocks_dev, jnp.int32)


def stack_rows(rows):
    n = rows[0].shape[1]
    row_id = lax.broadcasted_iota(jnp.int32, (GEO, n), 0)
    out = jnp.zeros((GEO, n), jnp.float32)
    for i, row in enumerate(rows):
        out = jnp.where(row_id == i, jnp.broadcast_to(row, (GEO, n)), out)
    return out


def table_kernel(cam, feats, means, conics, opac, table):
    bf16, f32 = jnp.bfloat16, jnp.float32

    def step(i, carry):
        at = pl.ds(i, 1)
        m = [means[k, at, :] for k in range(3)]
        screen = [
            cam[k, 0] * m[0] + cam[k, 1] * m[1] + cam[k, 2] * m[2] + cam[k, 3] for k in (0, 1)
        ]
        full = stack_rows(screen + [conics[k, at, :] for k in range(3)] + [opac[at, :]])
        hi = full.astype(bf16).astype(f32)
        rest = full - hi
        mid = rest.astype(bf16).astype(f32)
        low = rest - mid
        first = stack_rows([hi[k : k + 1] for k in range(6)] + [low[2:3], low[3:4]])
        second = stack_rows([mid[k : k + 1] for k in range(6)] + [low[4:5]])
        geo = jnp.concatenate([first, second], axis=0).astype(bf16)
        table[i] = jnp.concatenate([feats[i], geo], axis=0)
        return carry

    lax.fori_loop(0, feats.shape[0], step, 0, unroll=4)


def answer_kernel(asked, table, out, req, req_smem, sem):
    n = asked.shape[0]
    lane = lax.broadcasted_iota(jnp.int32, (1, n), 1)
    line = jnp.full((1, n), -1, jnp.int32)
    for i in range(n):
        line = jnp.where(lane == i, asked[i], line)
    req[...] = line
    copy = pltpu.make_async_copy(req, req_smem, sem)
    copy.start()
    copy.wait()

    def step(i, carry):
        out[i] = table[jnp.maximum(req_smem[0, i], 0)]
        return carry

    lax.fori_loop(0, n, step, 0, unroll=8)


def tile_kernel(
    blocks_dev, ids, cam, fetched, masks, cots, out,
    acc, abuf, ebuf, keeps, weights, flows, prefix, suffix, quad, quad_t, seen,
):
    tiles, channels, pixels = cots.shape
    side = math.isqrt(pixels)
    per_tile = ids.shape[0]
    n_scene, _, blk = fetched.shape
    rows = per_tile * blk
    half = rows // 2
    f32, bf16 = jnp.float32, jnp.bfloat16

    def dot(a, b):
        return jnp.dot(a, b, preferred_element_type=f32)

    ki = lax.broadcasted_iota(jnp.int32, (half, half), 0)
    ri = lax.broadcasted_iota(jnp.int32, (half, half), 1)
    one = jnp.ones((half, half), bf16)
    up = jnp.where(ki < ri, 1.0, 0.0).astype(bf16)
    prefix[:half] = one
    prefix[half:] = up
    suffix[:half] = jnp.where(ki > ri, 1.0, 0.0).astype(bf16)
    suffix[half:] = one

    def monomials(shape, pix_dim):
        pix = lax.broadcasted_iota(jnp.int32, shape, pix_dim)
        col = lax.broadcasted_iota(jnp.int32, shape, 1 - pix_dim) % GEO
        u = (pix % side).astype(f32) - 0.5 * (side - 1)
        w = (pix // side).astype(f32) - 0.5 * (side - 1)
        val = jnp.where(col == 0, 1.0, 0.0)
        for i, m in enumerate((u, w, u * u, u * w, w * w)):
            val = jnp.where(col == i + 1, m, val)
        return val.astype(bf16)

    quad[...] = monomials(quad.shape, 0)
    quad_t[...] = monomials(quad_t.shape, 1)

    def clear(i, carry):
        seen[i] = -1
        return carry

    lax.fori_loop(0, n_scene, clear, 0, unroll=8)

    def one_tile(t, n):
        slots = [lax.div(ids[j, t], blocks_dev) for j in range(per_tile)]
        parts = jnp.concatenate([fetched[s, channels:] for s in slots], axis=1).astype(f32)
        g = parts[:GEO] + parts[GEO:]
        sx, sy, op = g[0:1], g[1:2], g[5:6]
        a = g[2:3] + parts[6:7]
        b = g[3:4] + parts[7:8]
        c = g[4:5] + parts[14:15]
        live = masks[pl.ds(t, 1), :]
        ax_by = a * sx + b * sy
        bx_cy = b * sx + c * sy
        neg = jnp.exp(-op)
        log_sig = -jnp.log(1.0 + neg)
        one_less = neg / (1.0 + neg)
        const = log_sig - 0.5 * (sx * ax_by + sy * bx_cy)
        const = jnp.where(live > 0, const, -1e30)
        coef = stack_rows(
            [
                const,
                ax_by,
                bx_cy,
                -0.5 * a,
                -b,
                -0.5 * c,
            ]
        )
        hi = coef.astype(bf16).astype(f32)
        rest = coef - hi
        mid = rest.astype(bf16).astype(f32)
        coefs = jnp.concatenate([hi, mid, rest - mid, jnp.zeros_like(hi)], axis=0).astype(bf16)

        for q in (0, 1):
            cols = slice(q * half, (q + 1) * half)
            power = dot(quad[...], coefs[:, cols])
            alpha = jnp.exp(power)
            abuf[n, :, cols] = alpha
            keep = jnp.log(1.0 - alpha)
            keeps[n, :, cols] = keep.astype(bf16)
            ebuf[n, :, cols] = jnp.exp(power - keep)

        cot = cots[t]
        feat_rows = jnp.concatenate([fetched[s, :channels] for s in slots], axis=1)
        for q in (0, 1):
            cols = slice(q * half, (q + 1) * half)
            if q:
                before = dot(keeps[n], prefix[...])
            else:
                before = dot(keeps[n, :, :half], prefix[half:])
            weight = jnp.exp(before) * abuf[n, :, cols]
            weights[n, :, cols] = weight.astype(bf16)
            flow = weight * lax.dot_general(
                cot, feat_rows[:, cols], (((0,), (0,)), ((), ())), preferred_element_type=f32
            )
            abuf[n, :, cols] = flow
            flows[n, :, cols] = flow.astype(bf16)
        grad_feats = dot(cot, weights[n])
        for q in (0, 1):
            cols = slice(q * half, (q + 1) * half)
            if q:
                behind = dot(flows[n, :, half:], suffix[:half])
            else:
                behind = dot(flows[n], suffix[...])
            weights[n, :, cols] = (abuf[n, :, cols] - ebuf[n, :, cols] * behind).astype(bf16)
        mom = dot(quad_t[...], weights[n])
        m0, mu, mw, muu, muw, mww = [mom[i : i + 1] for i in range(6)]
        dx = mu - sx * m0
        dy = mw - sy * m0
        dxx = muu - sx * (mu + dx)
        dxy = muw - sx * mw - sy * dx
        dyy = mww - sy * (mw + dy)
        gsx = a * dx + b * dy
        gsy = b * dx + c * dy
        grad_geo = stack_rows(
            [
                cam[0, 0] * gsx + cam[1, 0] * gsy,
                cam[0, 1] * gsx + cam[1, 1] * gsy,
                cam[0, 2] * gsx + cam[1, 2] * gsy,
                -0.5 * dxx,
                -dxy,
                -0.5 * dyy,
                one_less * m0,
            ]
        )
        for j in range(per_tile):
            lanes = slice(j * blk, (j + 1) * blk)
            val = jnp.concatenate([grad_feats[:, lanes], grad_geo[:, lanes]], axis=0)
            mine = t * per_tile + j
            held = seen[slots[j]]
            at = jnp.where(held < 0, mine, held)
            seen[slots[j]] = at
            acc[at] = jnp.where(at == mine, val, acc[at] + val)

    def some_tiles(i, carry):
        for n in range(ABREAST):
            one_tile(i * ABREAST + n, n)
        return carry

    lax.fori_loop(0, tiles // ABREAST, some_tiles, 0)

    def give(t, carry):
        for j in range(per_tile):
            s = lax.div(ids[j, t], blocks_dev)
            out[s] = acc[seen[s]].astype(bf16)
        return carry

    lax.fori_loop(0, tiles, give, 0)


def owner_kernel(req, got, out, acc):
    views, blocks, out_rows, _ = out.shape
    share = out_rows - GEO
    acc[...] = jnp.zeros_like(acc)

    def step(i, carry):
        at = req[0, i]

        @pl.when(at >= 0)
        def _():
            acc[at] = acc[at] + got[i].astype(jnp.float32)

        return carry

    lax.fori_loop(0, got.shape[0], step, 0, unroll=4)

    def lay(i, carry):
        rows = acc[i].astype(jnp.bfloat16)
        for v in range(views):
            out[v, i] = jnp.concatenate(
                [rows[v * share : (v + 1) * share], rows[views * share :]], axis=0
            )
        return carry

    lax.fori_loop(0, blocks, lay, 0, unroll=4)


def view_kernel(got, out_feats, out_means, out_conics, out_opac):
    share = out_feats.shape[1]
    total = got[0].astype(jnp.float32)
    for v in range(1, got.shape[0]):
        total = total + got[v].astype(jnp.float32)
    out_feats[...] = total[:, :share]
    geo = total[:, share:]
    for k in range(3):
        out_means[k] = geo[:, k]
        out_conics[k] = geo[:, 3 + k]
    out_opac[...] = geo[:, 6]


def run_tiles(ids, cam, fetched, masks, cots, blocks_dev):
    n_scene, _, blk = fetched.shape
    tiles, channels, pixels = cots.shape
    entries = tiles * ids.shape[0]
    rows = ids.shape[0] * blk
    f32, bf16 = jnp.float32, jnp.bfloat16
    return call(
        lambda *refs: tile_kernel(blocks_dev, *refs),
        [jax.ShapeDtypeStruct((n_scene, channels + GEO, blk), bf16)],
        2, 3,
        scratch=[
            pltpu.VMEM((entries, channels + GEO, blk), f32),
            pltpu.VMEM((ABREAST, pixels, rows), f32),
            pltpu.VMEM((ABREAST, pixels, rows), f32),
            pltpu.VMEM((ABREAST, pixels, rows), bf16),
            pltpu.VMEM((ABREAST, pixels, rows), bf16),
            pltpu.VMEM((ABREAST, pixels, rows), bf16),
            pltpu.VMEM((rows, rows // 2), bf16),
            pltpu.VMEM((rows, rows // 2), bf16),
            pltpu.VMEM((pixels, 4 * GEO), bf16),
            pltpu.VMEM((2 * GEO, pixels), bf16),
            pltpu.SMEM((n_scene,), jnp.int32),
        ],
        name="tiles",
        mib=24,
    )(ids, cam, fetched, masks, cots)[0]


def body(features, means, conics, opacity, camera, lists, masks, cotangent):
    n_scene = lax.axis_size("scene")
    n_view = lax.axis_size("view")
    blocks_dev, channels, blk = features.shape
    f32, bf16, i32 = jnp.float32, jnp.bfloat16, jnp.int32
    cam = camera[0]
    ids = lists[0].T

    want = pl.pallas_call(
        lambda *refs: want_kernel(blocks_dev, *refs),
        out_shape=jax.ShapeDtypeStruct((n_scene, 1, n_scene), i32),
        in_specs=[pl.BlockSpec(memory_space=pltpu.MemorySpace.HBM)],
        out_specs=pl.BlockSpec(memory_space=VMEM),
        scratch_shapes=[pltpu.SMEM(ids.shape, i32), pltpu.SemaphoreType.DMA],
        name="want",
    )(ids)
    asked = lax.all_to_all(want, "scene", split_axis=0, concat_axis=0, tiled=True)
    width = channels + 2 * GEO
    (table,) = call(
        table_kernel, [jax.ShapeDtypeStruct((blocks_dev, width, blk), bf16)], 1, 4, name="table"
    )(cam, features, means.transpose(1, 0, 2), conics.transpose(1, 0, 2), opacity)
    answers, req = call(
        answer_kernel,
        [
            jax.ShapeDtypeStruct((n_scene, width, blk), bf16),
            jax.ShapeDtypeStruct((1, n_scene), i32),
        ],
        0, 2,
        scratch=[pltpu.SMEM((1, n_scene), i32), pltpu.SemaphoreType.DMA],
        name="answer",
    )(asked, table)
    fetched = lax.all_to_all(answers, "scene", split_axis=0, concat_axis=0, tiled=True)
    grads_out = run_tiles(ids, cam, fetched, masks[0], cotangent[0], blocks_dev)
    grads_in = lax.all_to_all(grads_out, "scene", split_axis=0, concat_axis=0, tiled=True)

    share = channels // n_view
    (sums_out,) = call(
        owner_kernel,
        [jax.ShapeDtypeStruct((n_view, blocks_dev, share + GEO, blk), bf16)],
        1, 1,
        scratch=[pltpu.VMEM((blocks_dev, channels + GEO, blk), f32)],
        name="owner",
    )(req, grads_in)
    sums_in = lax.all_to_all(sums_out, "view", split_axis=0, concat_axis=0, tiled=True)
    grad_feats, grad_means, grad_conics, grad_opac = call(
        view_kernel,
        [
            jax.ShapeDtypeStruct((blocks_dev, share, blk), f32),
            jax.ShapeDtypeStruct((3, blocks_dev, blk), f32),
            jax.ShapeDtypeStruct((3, blocks_dev, blk), f32),
            jax.ShapeDtypeStruct((blocks_dev, blk), f32),
        ],
        0, 1, name="views",
    )(sums_in)
    return grad_feats, grad_means.transpose(1, 0, 2), grad_conics.transpose(1, 0, 2), grad_opac


def solution(mesh):
    return jax.shard_map(
        body,
        mesh=mesh,
        in_specs=(
            P("scene", None, None),
            P("scene", None, None),
            P("scene", None, None),
            P("scene", None),
            P("view", None, None),
            P("view", "scene", None),
            P("view", "scene", None),
            P("view", "scene", None, None),
        ),
        out_specs=(
            P("scene", "view", None),
            P("scene", None, None),
            P("scene", None, None),
            P("scene", None),
        ),
        check_vma=False,
    )
```

```python
import math

import jax
import jax.numpy as jnp
from jax import lax
from jax.experimental import pallas as pl
from jax.experimental.pallas import tpu as pltpu
from jax.sharding import PartitionSpec as P

VMEM = pltpu.MemorySpace.VMEM
SMEM = pltpu.MemorySpace.SMEM
GEO = 8
ABREAST = 8
SLOTS = 4


def call(kernel, outs, n_smem, n_vmem, scratch=(), name=None, mib=8):
    return pl.pallas_call(
        kernel,
        out_shape=outs,
        in_specs=[pl.BlockSpec(memory_space=SMEM)] * n_smem
        + [pl.BlockSpec(memory_space=VMEM)] * n_vmem,
        out_specs=[pl.BlockSpec(memory_space=VMEM)] * len(outs),
        scratch_shapes=scratch,
        compiler_params=pltpu.CompilerParams(vmem_limit_bytes=mib * 1024 * 1024),
        name=name,
    )


def want_kernel(blocks_dev, lists, want, ids, sem):
    copy = pltpu.make_async_copy(lists, ids, sem)
    copy.start()
    want[...] = jnp.full(want.shape, -1, jnp.int32)
    copy.wait()
    for j in range(ids.shape[0]):
        for t in range(ids.shape[1]):
            owner = lax.div(ids[j, t], blocks_dev)
            want[owner] = jnp.full((1, want.shape[2]), ids[j, t] - owner * blocks_dev, jnp.int32)


def stack_rows(rows):
    n = rows[0].shape[1]
    row_id = lax.broadcasted_iota(jnp.int32, (GEO, n), 0)
    out = jnp.zeros((GEO, n), jnp.float32)
    for i, row in enumerate(rows):
        out = jnp.where(row_id == i, jnp.broadcast_to(row, (GEO, n)), out)
    return out


def table_kernel(cam, feats, means, conics, opac, table):
    bf16, f32 = jnp.bfloat16, jnp.float32

    def step(i, carry):
        at = pl.ds(i, 1)
        m = [means[k, at, :] for k in range(3)]
        screen = [
            cam[k, 0] * m[0] + cam[k, 1] * m[1] + cam[k, 2] * m[2] + cam[k, 3] for k in (0, 1)
        ]
        full = stack_rows(screen + [conics[k, at, :] for k in range(3)] + [opac[at, :]])
        hi = full.astype(bf16).astype(f32)
        rest = full - hi
        mid = rest.astype(bf16).astype(f32)
        low = rest - mid
        first = stack_rows([hi[k : k + 1] for k in range(6)] + [low[2:3], low[3:4]])
        second = stack_rows([mid[k : k + 1] for k in range(6)] + [low[4:5]])
        geo = jnp.concatenate([first, second], axis=0).astype(bf16)
        table[i] = jnp.concatenate([feats[i], geo], axis=0)
        return carry

    lax.fori_loop(0, feats.shape[0], step, 0, unroll=4)


def answer_kernel(asked, table, out, req, req_smem, sem):
    n = asked.shape[0]
    lane = lax.broadcasted_iota(jnp.int32, (1, n), 1)
    line = jnp.full((1, n), -1, jnp.int32)
    for i in range(n):
        line = jnp.where(lane == i, asked[i], line)
    req[...] = line
    copy = pltpu.make_async_copy(req, req_smem, sem)
    copy.start()
    copy.wait()

    def step(i, carry):
        out[i] = table[jnp.maximum(req_smem[0, i], 0)]
        return carry

    lax.fori_loop(0, n, step, 0, unroll=8)


def tile_kernel(
    blocks_dev, ids, cam, fetched, masks, cots, out,
    acc, abuf, ebuf, keeps, weights, flows, prefix, suffix, quad, quad_t, seen,
):
    tiles, channels, pixels = cots.shape
    side = math.isqrt(pixels)
    per_tile = ids.shape[0]
    n_scene, _, blk = fetched.shape
    rows = per_tile * blk
    half = rows // 2
    f32, bf16 = jnp.float32, jnp.bfloat16

    def dot(a, b):
        return jnp.dot(a, b, preferred_element_type=f32)

    ki = lax.broadcasted_iota(jnp.int32, (half, half), 0)
    ri = lax.broadcasted_iota(jnp.int32, (half, half), 1)
    one = jnp.ones((half, half), bf16)
    up = jnp.where(ki < ri, 1.0, 0.0).astype(bf16)
    prefix[:half] = one
    prefix[half:] = up
    suffix[:half] = jnp.where(ki > ri, 1.0, 0.0).astype(bf16)
    suffix[half:] = one

    def monomials(shape, pix_dim):
        pix = lax.broadcasted_iota(jnp.int32, shape, pix_dim)
        col = lax.broadcasted_iota(jnp.int32, shape, 1 - pix_dim) % GEO
        u = (pix % side).astype(f32) - 0.5 * (side - 1)
        w = (pix // side).astype(f32) - 0.5 * (side - 1)
        val = jnp.where(col == 0, 1.0, 0.0)
        for i, m in enumerate((u, w, u * u, u * w, w * w)):
            val = jnp.where(col == i + 1, m, val)
        return val.astype(bf16)

    quad[...] = monomials(quad.shape, 0)
    quad_t[...] = monomials(quad_t.shape, 1)

    def clear(i, carry):
        seen[i] = -1
        return carry

    lax.fori_loop(0, n_scene, clear, 0, unroll=8)

    def one_tile(t, n):
        slots = [lax.div(ids[j, t], blocks_dev) for j in range(per_tile)]
        parts = jnp.concatenate([fetched[s, channels:] for s in slots], axis=1).astype(f32)
        g = parts[:GEO] + parts[GEO:]
        sx, sy, op = g[0:1], g[1:2], g[5:6]
        a = g[2:3] + parts[6:7]
        b = g[3:4] + parts[7:8]
        c = g[4:5] + parts[14:15]
        live = masks[pl.ds(t, 1), :]
        ax_by = a * sx + b * sy
        bx_cy = b * sx + c * sy
        neg = jnp.exp(-op)
        log_sig = -jnp.log(1.0 + neg)
        one_less = neg / (1.0 + neg)
        const = log_sig - 0.5 * (sx * ax_by + sy * bx_cy)
        const = jnp.where(live > 0, const, -1e30)
        coef = stack_rows(
            [
                const,
                ax_by,
                bx_cy,
                -0.5 * a,
                -b,
                -0.5 * c,
            ]
        )
        hi = coef.astype(bf16).astype(f32)
        rest = coef - hi
        mid = rest.astype(bf16).astype(f32)
        coefs = jnp.concatenate([hi, mid, rest - mid, jnp.zeros_like(hi)], axis=0).astype(bf16)

        for q in (0, 1):
            cols = slice(q * half, (q + 1) * half)
            yield
            power = dot(quad[...], coefs[:, cols])
            alpha = jnp.exp(power)
            abuf[n, :, cols] = alpha
            keep = jnp.log(1.0 - alpha)
            keeps[n, :, cols] = keep.astype(bf16)
            ebuf[n, :, cols] = jnp.exp(power - keep)

        cot = cots[t]
        feat_rows = jnp.concatenate([fetched[s, :channels] for s in slots], axis=1)
        for q in (0, 1):
            cols = slice(q * half, (q + 1) * half)
            yield
            if q:
                before = dot(keeps[n], prefix[...])
            else:
                before = dot(keeps[n, :, :half], prefix[half:])
            weight = jnp.exp(before) * abuf[n, :, cols]
            weights[n, :, cols] = weight.astype(bf16)
            flow = weight * lax.dot_general(
                cot, feat_rows[:, cols], (((0,), (0,)), ((), ())), preferred_element_type=f32
            )
            abuf[n, :, cols] = flow
            flows[n, :, cols] = flow.astype(bf16)
        yield
        grad_feats = dot(cot, weights[n])
        for q in (0, 1):
            cols = slice(q * half, (q + 1) * half)
            yield
            if q:
                behind = dot(flows[n, :, half:], suffix[:half])
            else:
                behind = dot(flows[n], suffix[...])
            weights[n, :, cols] = (abuf[n, :, cols] - ebuf[n, :, cols] * behind).astype(bf16)
        yield
        mom = dot(quad_t[...], weights[n])
        m0, mu, mw, muu, muw, mww = [mom[i : i + 1] for i in range(6)]
        dx = mu - sx * m0
        dy = mw - sy * m0
        dxx = muu - sx * (mu + dx)
        dxy = muw - sx * mw - sy * dx
        dyy = mww - sy * (mw + dy)
        gsx = a * dx + b * dy
        gsy = b * dx + c * dy
        grad_geo = stack_rows(
            [
                cam[0, 0] * gsx + cam[1, 0] * gsy,
                cam[0, 1] * gsx + cam[1, 1] * gsy,
                cam[0, 2] * gsx + cam[1, 2] * gsy,
                -0.5 * dxx,
                -dxy,
                -0.5 * dyy,
                one_less * m0,
            ]
        )
        for j in range(per_tile):
            lanes = slice(j * blk, (j + 1) * blk)
            val = jnp.concatenate([grad_feats[:, lanes], grad_geo[:, lanes]], axis=0)
            mine = t * per_tile + j
            held = seen[slots[j]]
            at = jnp.where(held < 0, mine, held)
            seen[slots[j]] = at
            acc[at] = jnp.where(at == mine, val, acc[at] + val)

    def some_tiles(i, carry):
        waiting = [one_tile(i * ABREAST + n, n % SLOTS) for n in range(ABREAST)]
        runs = []
        while waiting or runs:
            runs += waiting[:1]
            del waiting[:1]
            for _ in range(2):
                runs = [run for run in runs if next(run, run) is None]
        return carry

    lax.fori_loop(0, tiles // ABREAST, some_tiles, 0)

    def give(t, carry):
        for j in range(per_tile):
            s = lax.div(ids[j, t], blocks_dev)
            out[s] = acc[seen[s]].astype(bf16)
        return carry

    lax.fori_loop(0, tiles, give, 0)


def owner_kernel(req, got, out, acc):
    views, blocks, out_rows, _ = out.shape
    share = out_rows - GEO
    acc[...] = jnp.zeros_like(acc)

    def step(i, carry):
        at = req[0, i]

        @pl.when(at >= 0)
        def _():
            acc[at] = acc[at] + got[i].astype(jnp.float32)

        return carry

    lax.fori_loop(0, got.shape[0], step, 0, unroll=4)

    def lay(i, carry):
        rows = acc[i].astype(jnp.bfloat16)
        for v in range(views):
            out[v, i] = jnp.concatenate(
                [rows[v * share : (v + 1) * share], rows[views * share :]], axis=0
            )
        return carry

    lax.fori_loop(0, blocks, lay, 0, unroll=4)


def view_kernel(got, out_feats, out_means, out_conics, out_opac):
    share = out_feats.shape[1]
    total = got[0].astype(jnp.float32)
    for v in range(1, got.shape[0]):
        total = total + got[v].astype(jnp.float32)
    out_feats[...] = total[:, :share]
    geo = total[:, share:]
    for k in range(3):
        out_means[k] = geo[:, k]
        out_conics[k] = geo[:, 3 + k]
    out_opac[...] = geo[:, 6]


def run_tiles(ids, cam, fetched, masks, cots, blocks_dev):
    n_scene, _, blk = fetched.shape
    tiles, channels, pixels = cots.shape
    entries = tiles * ids.shape[0]
    rows = ids.shape[0] * blk
    f32, bf16 = jnp.float32, jnp.bfloat16
    return call(
        lambda *refs: tile_kernel(blocks_dev, *refs),
        [jax.ShapeDtypeStruct((n_scene, channels + GEO, blk), bf16)],
        2, 3,
        scratch=[
            pltpu.VMEM((entries, channels + GEO, blk), f32),
            pltpu.VMEM((SLOTS, pixels, rows), f32),
            pltpu.VMEM((SLOTS, pixels, rows), f32),
            pltpu.VMEM((SLOTS, pixels, rows), bf16),
            pltpu.VMEM((SLOTS, pixels, rows), bf16),
            pltpu.VMEM((SLOTS, pixels, rows), bf16),
            pltpu.VMEM((rows, rows // 2), bf16),
            pltpu.VMEM((rows, rows // 2), bf16),
            pltpu.VMEM((pixels, 4 * GEO), bf16),
            pltpu.VMEM((2 * GEO, pixels), bf16),
            pltpu.SMEM((n_scene,), jnp.int32),
        ],
        name="tiles",
        mib=24,
    )(ids, cam, fetched, masks, cots)[0]


def body(features, means, conics, opacity, camera, lists, masks, cotangent):
    n_scene = lax.axis_size("scene")
    n_view = lax.axis_size("view")
    blocks_dev, channels, blk = features.shape
    f32, bf16, i32 = jnp.float32, jnp.bfloat16, jnp.int32
    cam = camera[0]
    ids = lists[0].T

    want = pl.pallas_call(
        lambda *refs: want_kernel(blocks_dev, *refs),
        out_shape=jax.ShapeDtypeStruct((n_scene, 1, n_scene), i32),
        in_specs=[pl.BlockSpec(memory_space=pltpu.MemorySpace.HBM)],
        out_specs=pl.BlockSpec(memory_space=VMEM),
        scratch_shapes=[pltpu.SMEM(ids.shape, i32), pltpu.SemaphoreType.DMA],
        name="want",
    )(ids)
    asked = lax.all_to_all(want, "scene", split_axis=0, concat_axis=0, tiled=True)
    width = channels + 2 * GEO
    (table,) = call(
        table_kernel, [jax.ShapeDtypeStruct((blocks_dev, width, blk), bf16)], 1, 4, name="table"
    )(cam, features, means.transpose(1, 0, 2), conics.transpose(1, 0, 2), opacity)
    answers, req = call(
        answer_kernel,
        [
            jax.ShapeDtypeStruct((n_scene, width, blk), bf16),
            jax.ShapeDtypeStruct((1, n_scene), i32),
        ],
        0, 2,
        scratch=[pltpu.SMEM((1, n_scene), i32), pltpu.SemaphoreType.DMA],
        name="answer",
    )(asked, table)
    fetched = lax.all_to_all(answers, "scene", split_axis=0, concat_axis=0, tiled=True)
    grads_out = run_tiles(ids, cam, fetched, masks[0], cotangent[0], blocks_dev)
    grads_in = lax.all_to_all(grads_out, "scene", split_axis=0, concat_axis=0, tiled=True)

    share = channels // n_view
    (sums_out,) = call(
        owner_kernel,
        [jax.ShapeDtypeStruct((n_view, blocks_dev, share + GEO, blk), bf16)],
        1, 1,
        scratch=[pltpu.VMEM((blocks_dev, channels + GEO, blk), f32)],
        name="owner",
    )(req, grads_in)
    sums_in = lax.all_to_all(sums_out, "view", split_axis=0, concat_axis=0, tiled=True)
    grad_feats, grad_means, grad_conics, grad_opac = call(
        view_kernel,
        [
            jax.ShapeDtypeStruct((blocks_dev, share, blk), f32),
            jax.ShapeDtypeStruct((3, blocks_dev, blk), f32),
            jax.ShapeDtypeStruct((3, blocks_dev, blk), f32),
            jax.ShapeDtypeStruct((blocks_dev, blk), f32),
        ],
        0, 1, name="views",
    )(sums_in)
    return grad_feats, grad_means.transpose(1, 0, 2), grad_conics.transpose(1, 0, 2), grad_opac


def solution(mesh):
    return jax.shard_map(
        body,
        mesh=mesh,
        in_specs=(
            P("scene", None, None),
            P("scene", None, None),
            P("scene", None, None),
            P("scene", None),
            P("view", None, None),
            P("view", "scene", None),
            P("view", "scene", None),
            P("view", "scene", None, None),
        ),
        out_specs=(
            P("scene", "view", None),
            P("scene", None, None),
            P("scene", None, None),
            P("scene", None),
        ),
        check_vma=False,
    )
```

```python
import math

import jax
import jax.numpy as jnp
from jax import lax
from jax.experimental import pallas as pl
from jax.experimental.pallas import tpu as pltpu
from jax.sharding import PartitionSpec as P

VMEM = pltpu.MemorySpace.VMEM
SMEM = pltpu.MemorySpace.SMEM
LOG2E = math.log2(math.e)
GEO = 8
LINE = 16
ABREAST = 8
SLOTS = 4


def call(kernel, outs, n_smem, n_vmem, scratch=(), name=None, mib=8):
    return pl.pallas_call(
        kernel,
        out_shape=outs,
        in_specs=[pl.BlockSpec(memory_space=SMEM)] * n_smem
        + [pl.BlockSpec(memory_space=VMEM)] * n_vmem,
        out_specs=[pl.BlockSpec(memory_space=VMEM)] * len(outs),
        scratch_shapes=scratch,
        compiler_params=pltpu.CompilerParams(vmem_limit_bytes=mib * 1024 * 1024),
        name=name,
    )


def want_kernel(blocks_dev, lists, want, ids, sem):
    copy = pltpu.make_async_copy(lists, ids, sem)
    copy.start()
    want[...] = jnp.full(want.shape, -1, jnp.int32)
    copy.wait()
    for j in range(ids.shape[0]):
        for t in range(ids.shape[1]):
            owner = lax.div(ids[j, t], blocks_dev)
            line = lax.div(owner, want.shape[0])
            want[owner - line * want.shape[0], pl.ds(line, 1), :] = jnp.full(
                (1, want.shape[2]), ids[j, t] - owner * blocks_dev, jnp.int32
            )


def turn_kernel(asked, out):
    lane = lax.broadcasted_iota(jnp.int32, asked.shape[1:], 1)
    rows = asked[0]
    for i in range(1, asked.shape[0]):
        rows = jnp.where(lane == i, asked[i], rows)
    for k in range(out.shape[0]):
        out[k] = rows[k : k + 1]


def stack_rows(rows):
    n = rows[0].shape[1]
    row_id = lax.broadcasted_iota(jnp.int32, (GEO, n), 0)
    out = jnp.zeros((GEO, n), jnp.float32)
    for i, row in enumerate(rows):
        out = jnp.where(row_id == i, jnp.broadcast_to(row, (GEO, n)), out)
    return out


def table_kernel(*refs):
    far, table, near, sems = refs[:5], refs[5], refs[6:11], refs[11]
    copies = [pltpu.make_async_copy(*pair, sems.at[k]) for k, pair in enumerate(zip(far, near))]
    for copy in copies:
        copy.start()
    for copy in copies:
        copy.wait()
    cam, feats, means, conics, opac = near
    bf16, f32 = jnp.bfloat16, jnp.float32

    def step(i, carry):
        at = pl.ds(i, 1)
        m = [means[k, at, :] for k in range(3)]
        screen = [
            cam[k, 0] * m[0] + cam[k, 1] * m[1] + cam[k, 2] * m[2] + cam[k, 3] for k in (0, 1)
        ]
        full = stack_rows(screen + [conics[k, at, :] for k in range(3)] + [opac[at, :]])
        hi = full.astype(bf16).astype(f32)
        rest = full - hi
        mid = rest.astype(bf16).astype(f32)
        low = rest - mid
        first = stack_rows([hi[k : k + 1] for k in range(6)] + [low[2:3], low[3:4]])
        second = stack_rows([mid[k : k + 1] for k in range(6)] + [low[4:5]])
        geo = jnp.concatenate([first, second], axis=0).astype(bf16)
        table[i] = jnp.concatenate([feats[i], geo], axis=0)
        return carry

    lax.fori_loop(0, feats.shape[0], step, 0, unroll=4)


def answer_kernel(req, table, out):
    lines = req.shape[0]
    line_len = out.shape[0] // lines

    def step(i, carry):
        line = lax.div(i, line_len)
        out[i] = table[jnp.maximum(req[line, 0, i - line * line_len], 0)]
        return carry

    lax.fori_loop(0, out.shape[0], step, 0, unroll=8)


def tile_kernel(
    blocks_dev, ids, cam, fetched, masks, cots, out,
    acc, abuf, ebuf, keeps, weights, flows, prefix, suffix, quad, quad_t, seen,
):
    tiles, channels, pixels = cots.shape
    side = math.isqrt(pixels)
    per_tile = ids.shape[0]
    n_scene, _, blk = fetched.shape
    rows = per_tile * blk
    half = rows // 2
    f32, bf16 = jnp.float32, jnp.bfloat16

    def dot(a, b):
        return jnp.dot(a, b, preferred_element_type=f32)

    ki = lax.broadcasted_iota(jnp.int32, (half, half), 0)
    ri = lax.broadcasted_iota(jnp.int32, (half, half), 1)
    one = jnp.ones((half, half), bf16)
    up = jnp.where(ki < ri, 1.0, 0.0).astype(bf16)
    prefix[:half] = one
    prefix[half:] = up
    suffix[:half] = jnp.where(ki > ri, 1.0, 0.0).astype(bf16)
    suffix[half:] = one

    def monomials(shape, pix_dim):
        pix = lax.broadcasted_iota(jnp.int32, shape, pix_dim)
        col = lax.broadcasted_iota(jnp.int32, shape, 1 - pix_dim) % GEO
        u = (pix % side).astype(f32) - 0.5 * (side - 1)
        w = (pix // side).astype(f32) - 0.5 * (side - 1)
        val = jnp.where(col == 0, 1.0, 0.0)
        for i, m in enumerate((u, w, u * u, u * w, w * w)):
            val = jnp.where(col == i + 1, m, val)
        return val.astype(bf16)

    quad[...] = monomials(quad.shape, 0)
    quad_t[...] = monomials(quad_t.shape, 1)

    def clear(i, carry):
        seen[i] = -1
        return carry

    lax.fori_loop(0, n_scene, clear, 0, unroll=8)

    def one_tile(t, n):
        slots = [lax.div(ids[j, t], blocks_dev) for j in range(per_tile)]
        parts = jnp.concatenate([fetched[s, channels:] for s in slots], axis=1).astype(f32)
        g = parts[:GEO] + parts[GEO:]
        sx, sy, op = g[0:1], g[1:2], g[5:6]
        a = g[2:3] + parts[6:7]
        b = g[3:4] + parts[7:8]
        c = g[4:5] + parts[14:15]
        live = masks[pl.ds(t, 1), :]
        ax_by = a * sx + b * sy
        bx_cy = b * sx + c * sy
        neg = jnp.exp(-op)
        log_sig = -jnp.log(1.0 + neg)
        one_less = neg / (1.0 + neg)
        const = log_sig - 0.5 * (sx * ax_by + sy * bx_cy)
        const = jnp.where(live > 0, const * LOG2E, -1e30)
        coef = stack_rows(
            [
                const,
                ax_by * LOG2E,
                bx_cy * LOG2E,
                a * (-0.5 * LOG2E),
                b * (-LOG2E),
                c * (-0.5 * LOG2E),
            ]
        )
        hi = coef.astype(bf16).astype(f32)
        rest = coef - hi
        mid = rest.astype(bf16).astype(f32)
        coefs = jnp.concatenate([hi, mid, rest - mid, jnp.zeros_like(hi)], axis=0).astype(bf16)

        for q in (0, 1):
            cols = slice(q * half, (q + 1) * half)
            yield
            power = dot(quad[...], coefs[:, cols])
            alpha = jnp.exp2(power)
            abuf[n, :, cols] = alpha
            keep = jnp.log(1.0 - alpha) * LOG2E
            keeps[n, :, cols] = keep.astype(bf16)
            ebuf[n, :, cols] = jnp.exp2(power - keep)

        cot = cots[t]
        feat_rows = jnp.concatenate([fetched[s, :channels] for s in slots], axis=1)
        for q in (0, 1):
            cols = slice(q * half, (q + 1) * half)
            yield
            if q:
                before = dot(keeps[n], prefix[...])
            else:
                before = dot(keeps[n, :, :half], prefix[half:])
            weight = jnp.exp2(before) * abuf[n, :, cols]
            weights[n, :, cols] = weight.astype(bf16)
            flow = weight * lax.dot_general(
                cot, feat_rows[:, cols], (((0,), (0,)), ((), ())), preferred_element_type=f32
            )
            abuf[n, :, cols] = flow
            flows[n, :, cols] = flow.astype(bf16)
        yield
        grad_feats = dot(cot, weights[n])
        for q in (0, 1):
            cols = slice(q * half, (q + 1) * half)
            yield
            if q:
                behind = dot(flows[n, :, half:], suffix[:half])
            else:
                behind = dot(flows[n], suffix[...])
            weights[n, :, cols] = (abuf[n, :, cols] - ebuf[n, :, cols] * behind).astype(bf16)
        yield
        mom = dot(quad_t[...], weights[n])
        m0, mu, mw, muu, muw, mww = [mom[i : i + 1] for i in range(6)]
        dx = mu - sx * m0
        dy = mw - sy * m0
        dxx = muu - sx * (mu + dx)
        dxy = muw - sx * mw - sy * dx
        dyy = mww - sy * (mw + dy)
        gsx = a * dx + b * dy
        gsy = b * dx + c * dy
        grad_geo = stack_rows(
            [
                cam[0, 0] * gsx + cam[1, 0] * gsy,
                cam[0, 1] * gsx + cam[1, 1] * gsy,
                cam[0, 2] * gsx + cam[1, 2] * gsy,
                -0.5 * dxx,
                -dxy,
                -0.5 * dyy,
                one_less * m0,
            ]
        )
        for j in range(per_tile):
            lanes = slice(j * blk, (j + 1) * blk)
            val = jnp.concatenate([grad_feats[:, lanes], grad_geo[:, lanes]], axis=0)
            mine = t * per_tile + j
            held = seen[slots[j]]
            at = jnp.where(held < 0, mine, held)
            seen[slots[j]] = at
            acc[at] = jnp.where(at == mine, val, acc[at] + val)

    def some_tiles(i, carry):
        waiting = [one_tile(i * ABREAST + n, n % SLOTS) for n in range(ABREAST)]
        runs = []
        while waiting or runs:
            runs += waiting[:1]
            del waiting[:1]
            for _ in range(2):
                runs = [run for run in runs if next(run, run) is None]
        return carry

    lax.fori_loop(0, tiles // ABREAST, some_tiles, 0)

    def give(t, carry):
        for j in range(per_tile):
            s = lax.div(ids[j, t], blocks_dev)
            out[s] = acc[seen[s]].astype(bf16)
        return carry

    lax.fori_loop(0, tiles, give, 0)


def owner_kernel(req, got, out, acc):
    views, blocks, out_rows, _ = out.shape
    share = out_rows - GEO
    lines = req.shape[0]
    line_len = got.shape[0] // lines
    acc[...] = jnp.zeros_like(acc)

    def step(i, carry):
        line = lax.div(i, line_len)
        at = req[line, 0, i - line * line_len]

        @pl.when(at >= 0)
        def _():
            acc[at] = acc[at] + got[i].astype(jnp.float32)

        return carry

    lax.fori_loop(0, got.shape[0], step, 0, unroll=4)

    def lay(i, carry):
        rows = acc[i].astype(jnp.bfloat16)
        for v in range(views):
            out[v, i] = jnp.concatenate(
                [rows[v * share : (v + 1) * share], rows[views * share :]], axis=0
            )
        return carry

    lax.fori_loop(0, blocks, lay, 0, unroll=4)


def view_kernel(got, out_feats, out_means, out_conics, out_opac):
    share = out_feats.shape[1]
    total = got[0].astype(jnp.float32)
    for v in range(1, got.shape[0]):
        total = total + got[v].astype(jnp.float32)
    out_feats[...] = total[:, :share]
    geo = total[:, share:]
    for k in range(3):
        out_means[k] = geo[:, k]
        out_conics[k] = geo[:, 3 + k]
    out_opac[...] = geo[:, 6]


def run_tiles(ids, cam, fetched, masks, cots, blocks_dev):
    n_scene, _, blk = fetched.shape
    tiles, channels, pixels = cots.shape
    entries = tiles * ids.shape[0]
    rows = ids.shape[0] * blk
    f32, bf16 = jnp.float32, jnp.bfloat16
    return call(
        lambda *refs: tile_kernel(blocks_dev, *refs),
        [jax.ShapeDtypeStruct((n_scene, channels + GEO, blk), bf16)],
        2, 3,
        scratch=[
            pltpu.VMEM((entries, channels + GEO, blk), f32),
            pltpu.VMEM((SLOTS, pixels, rows), f32),
            pltpu.VMEM((SLOTS, pixels, rows), f32),
            pltpu.VMEM((SLOTS, pixels, rows), bf16),
            pltpu.VMEM((SLOTS, pixels, rows), bf16),
            pltpu.VMEM((SLOTS, pixels, rows), bf16),
            pltpu.VMEM((rows, rows // 2), bf16),
            pltpu.VMEM((rows, rows // 2), bf16),
            pltpu.VMEM((pixels, 4 * GEO), bf16),
            pltpu.VMEM((2 * GEO, pixels), bf16),
            pltpu.SMEM((n_scene,), jnp.int32),
        ],
        name="tiles",
        mib=24,
    )(ids, cam, fetched, masks, cots)[0]


def body(features, means, conics, opacity, camera, lists, masks, cotangent):
    n_scene = lax.axis_size("scene")
    n_view = lax.axis_size("view")
    blocks_dev, channels, blk = features.shape
    f32, bf16, i32 = jnp.float32, jnp.bfloat16, jnp.int32
    cam = camera[0]
    ids = lists[0].T

    want = pl.pallas_call(
        lambda *refs: want_kernel(blocks_dev, *refs),
        out_shape=jax.ShapeDtypeStruct((LINE, n_scene // LINE, blk), i32),
        in_specs=[pl.BlockSpec(memory_space=pltpu.MemorySpace.HBM)],
        out_specs=pl.BlockSpec(memory_space=VMEM),
        scratch_shapes=[pltpu.SMEM(ids.shape, i32), pltpu.SemaphoreType.DMA],
        name="want",
    )(ids)
    lines = n_scene // LINE
    along = [[k * LINE + i for i in range(LINE)] for k in range(lines)]
    across = [[k * LINE + i for k in range(lines)] for i in range(LINE)]
    asked = lax.all_to_all(
        want, "scene", split_axis=0, concat_axis=0, tiled=True, axis_index_groups=along
    )
    (turned,) = call(
        turn_kernel, [jax.ShapeDtypeStruct((lines, 1, blk), i32)], 0, 1, name="turn"
    )(asked)
    req = lax.all_to_all(
        turned, "scene", split_axis=0, concat_axis=0, tiled=True, axis_index_groups=across
    )
    width = channels + 2 * GEO
    sources = (cam, features, means.transpose(1, 0, 2), conics.transpose(1, 0, 2), opacity)
    table = pl.pallas_call(
        table_kernel,
        out_shape=jax.ShapeDtypeStruct((blocks_dev, width, blk), bf16),
        in_specs=[pl.BlockSpec(memory_space=pltpu.MemorySpace.HBM)] * len(sources),
        out_specs=pl.BlockSpec(memory_space=VMEM),
        scratch_shapes=[pltpu.SMEM(cam.shape, f32)]
        + [pltpu.VMEM(x.shape, x.dtype) for x in sources[1:]]
        + [pltpu.SemaphoreType.DMA((len(sources),))],
        compiler_params=pltpu.CompilerParams(vmem_limit_bytes=60 * 1024 * 1024),
        name="table",
    )(*sources)
    (answers,) = call(
        answer_kernel, [jax.ShapeDtypeStruct((n_scene, width, blk), bf16)], 1, 1, name="answer"
    )(req, table)
    fetched = lax.all_to_all(answers, "scene", split_axis=0, concat_axis=0, tiled=True)
    grads_out = run_tiles(ids, cam, fetched, masks[0], cotangent[0], blocks_dev)
    grads_in = lax.all_to_all(grads_out, "scene", split_axis=0, concat_axis=0, tiled=True)

    share = channels // n_view
    (sums_out,) = call(
        owner_kernel,
        [jax.ShapeDtypeStruct((n_view, blocks_dev, share + GEO, blk), bf16)],
        1, 1,
        scratch=[pltpu.VMEM((blocks_dev, channels + GEO, blk), f32)],
        name="owner",
    )(req, grads_in)
    sums_in = lax.all_to_all(sums_out, "view", split_axis=0, concat_axis=0, tiled=True)
    grad_feats, grad_means, grad_conics, grad_opac = call(
        view_kernel,
        [
            jax.ShapeDtypeStruct((blocks_dev, share, blk), f32),
            jax.ShapeDtypeStruct((3, blocks_dev, blk), f32),
            jax.ShapeDtypeStruct((3, blocks_dev, blk), f32),
            jax.ShapeDtypeStruct((blocks_dev, blk), f32),
        ],
        0, 1, name="views",
    )(sums_in)
    return grad_feats, grad_means.transpose(1, 0, 2), grad_conics.transpose(1, 0, 2), grad_opac


def solution(mesh):
    return jax.shard_map(
        body,
        mesh=mesh,
        in_specs=(
            P("scene", None, None),
            P("scene", None, None),
            P("scene", None, None),
            P("scene", None),
            P("view", None, None),
            P("view", "scene", None),
            P("view", "scene", None),
            P("view", "scene", None, None),
        ),
        out_specs=(
            P("scene", "view", None),
            P("scene", None, None),
            P("scene", None, None),
            P("scene", None),
        ),
        check_vma=False,
    )
```

```python
import math

import jax
import jax.numpy as jnp
from jax import lax
from jax.experimental import pallas as pl
from jax.experimental.pallas import tpu as pltpu
from jax.sharding import PartitionSpec as P

VMEM = pltpu.MemorySpace.VMEM
SMEM = pltpu.MemorySpace.SMEM
LOG2E = math.log2(math.e)
GEO = 8
ABREAST = 8
SLOTS = 4


def call(kernel, outs, n_smem, n_vmem, scratch=(), name=None, mib=8):
    return pl.pallas_call(
        kernel,
        out_shape=outs,
        in_specs=[pl.BlockSpec(memory_space=SMEM)] * n_smem
        + [pl.BlockSpec(memory_space=VMEM)] * n_vmem,
        out_specs=[pl.BlockSpec(memory_space=VMEM)] * len(outs),
        scratch_shapes=scratch,
        compiler_params=pltpu.CompilerParams(vmem_limit_bytes=mib * 1024 * 1024),
        name=name,
    )


def want_kernel(blocks_dev, lists, want, ids, sem):
    copy = pltpu.make_async_copy(lists, ids, sem)
    copy.start()
    want[...] = jnp.full(want.shape, -1, jnp.int32)
    copy.wait()
    for j in range(ids.shape[0]):
        for t in range(ids.shape[1]):
            owner = lax.div(ids[j, t], blocks_dev)
            want[owner] = jnp.full((1, want.shape[2]), ids[j, t] - owner * blocks_dev, jnp.int32)


def stack_rows(rows):
    n = rows[0].shape[1]
    row_id = lax.broadcasted_iota(jnp.int32, (GEO, n), 0)
    out = jnp.zeros((GEO, n), jnp.float32)
    for i, row in enumerate(rows):
        out = jnp.where(row_id == i, jnp.broadcast_to(row, (GEO, n)), out)
    return out


def table_kernel(cam, feats, means, conics, opac, table):
    bf16, f32 = jnp.bfloat16, jnp.float32

    def step(i, carry):
        at = pl.ds(i, 1)
        m = [means[k, at, :] for k in range(3)]
        screen = [
            cam[k, 0] * m[0] + cam[k, 1] * m[1] + cam[k, 2] * m[2] + cam[k, 3] for k in (0, 1)
        ]
        full = stack_rows(screen + [conics[k, at, :] for k in range(3)] + [opac[at, :]])
        hi = full.astype(bf16).astype(f32)
        rest = full - hi
        mid = rest.astype(bf16).astype(f32)
        low = rest - mid
        first = stack_rows([hi[k : k + 1] for k in range(6)] + [low[2:3], low[3:4]])
        second = stack_rows([mid[k : k + 1] for k in range(6)] + [low[4:5]])
        geo = jnp.concatenate([first, second], axis=0).astype(bf16)
        table[i] = jnp.concatenate([feats[i], geo], axis=0)
        return carry

    lax.fori_loop(0, feats.shape[0], step, 0, unroll=4)


def answer_kernel(view, asked, table, out, req, req_smem, sem):
    n = asked.shape[0]
    lane = lax.broadcasted_iota(jnp.int32, (1, n), 1)
    line = jnp.full((1, n), -1, jnp.int32)
    for i in range(n):
        line = jnp.where(lane == i, asked[i], line)
    req[0] = line
    req[1] = jnp.full((1, n), view[0], jnp.int32)
    copy = pltpu.make_async_copy(req.at[0], req_smem, sem)
    copy.start()
    copy.wait()

    def step(i, carry):
        out[i] = table[jnp.maximum(req_smem[0, i], 0)]
        return carry

    lax.fori_loop(0, n, step, 0, unroll=8)


def tile_kernel(
    blocks_dev, ids, cam, fetched, masks, cots, out,
    acc, abuf, ebuf, keeps, weights, flows, prefix, suffix, quad, quad_t, seen,
):
    tiles, channels, pixels = cots.shape
    side = math.isqrt(pixels)
    per_tile = ids.shape[0]
    n_scene, _, blk = fetched.shape
    rows = per_tile * blk
    half = rows // 2
    f32, bf16 = jnp.float32, jnp.bfloat16

    def dot(a, b):
        return jnp.dot(a, b, preferred_element_type=f32)

    ki = lax.broadcasted_iota(jnp.int32, (half, half), 0)
    ri = lax.broadcasted_iota(jnp.int32, (half, half), 1)
    one = jnp.ones((half, half), bf16)
    up = jnp.where(ki < ri, 1.0, 0.0).astype(bf16)
    prefix[:half] = one
    prefix[half:] = up
    suffix[:half] = jnp.where(ki > ri, 1.0, 0.0).astype(bf16)
    suffix[half:] = one

    def monomials(shape, pix_dim):
        pix = lax.broadcasted_iota(jnp.int32, shape, pix_dim)
        col = lax.broadcasted_iota(jnp.int32, shape, 1 - pix_dim) % GEO
        u = (pix % side).astype(f32) - 0.5 * (side - 1)
        w = (pix // side).astype(f32) - 0.5 * (side - 1)
        val = jnp.where(col == 0, 1.0, 0.0)
        for i, m in enumerate((u, w, u * u, u * w, w * w)):
            val = jnp.where(col == i + 1, m, val)
        return val.astype(bf16)

    quad[...] = monomials(quad.shape, 0)
    quad_t[...] = monomials(quad_t.shape, 1)

    def clear(i, carry):
        seen[i] = -1
        return carry

    lax.fori_loop(0, n_scene, clear, 0, unroll=8)

    def one_tile(t, n):
        slots = [lax.div(ids[j, t], blocks_dev) for j in range(per_tile)]
        parts = jnp.concatenate([fetched[s, channels:] for s in slots], axis=1).astype(f32)
        g = parts[:GEO] + parts[GEO:]
        sx, sy, op = g[0:1], g[1:2], g[5:6]
        a = g[2:3] + parts[6:7]
        b = g[3:4] + parts[7:8]
        c = g[4:5] + parts[14:15]
        live = masks[pl.ds(t, 1), :]
        ax_by = a * sx + b * sy
        bx_cy = b * sx + c * sy
        neg = jnp.exp(-op)
        log_sig = -jnp.log(1.0 + neg)
        one_less = neg / (1.0 + neg)
        const = log_sig - 0.5 * (sx * ax_by + sy * bx_cy)
        const = jnp.where(live > 0, const * LOG2E, -1e30)
        coef = stack_rows(
            [
                const,
                ax_by * LOG2E,
                bx_cy * LOG2E,
                a * (-0.5 * LOG2E),
                b * (-LOG2E),
                c * (-0.5 * LOG2E),
            ]
        )
        hi = coef.astype(bf16).astype(f32)
        rest = coef - hi
        mid = rest.astype(bf16).astype(f32)
        coefs = jnp.concatenate([hi, mid, rest - mid, jnp.zeros_like(hi)], axis=0).astype(bf16)

        for q in (0, 1):
            cols = slice(q * half, (q + 1) * half)
            yield
            power = dot(quad[...], coefs[:, cols])
            alpha = jnp.exp2(power)
            abuf[n, :, cols] = alpha
            keep = jnp.log(1.0 - alpha) * LOG2E
            keeps[n, :, cols] = keep.astype(bf16)
            ebuf[n, :, cols] = jnp.exp2(power - keep)

        cot = cots[t]
        feat_rows = jnp.concatenate([fetched[s, :channels] for s in slots], axis=1)
        for q in (0, 1):
            cols = slice(q * half, (q + 1) * half)
            yield
            if q:
                before = dot(keeps[n], prefix[...])
            else:
                before = dot(keeps[n, :, :half], prefix[half:])
            weight = jnp.exp2(before) * abuf[n, :, cols]
            weights[n, :, cols] = weight.astype(bf16)
            flow = weight * lax.dot_general(
                cot, feat_rows[:, cols], (((0,), (0,)), ((), ())), preferred_element_type=f32
            )
            abuf[n, :, cols] = flow
            flows[n, :, cols] = flow.astype(bf16)
        yield
        grad_feats = dot(cot, weights[n])
        for q in (0, 1):
            cols = slice(q * half, (q + 1) * half)
            yield
            if q:
                behind = dot(flows[n, :, half:], suffix[:half])
            else:
                behind = dot(flows[n], suffix[...])
            weights[n, :, cols] = (abuf[n, :, cols] - ebuf[n, :, cols] * behind).astype(bf16)
        yield
        mom = dot(quad_t[...], weights[n])
        m0, mu, mw, muu, muw, mww = [mom[i : i + 1] for i in range(6)]
        dx = mu - sx * m0
        dy = mw - sy * m0
        dxx = muu - sx * (mu + dx)
        dxy = muw - sx * mw - sy * dx
        dyy = mww - sy * (mw + dy)
        gsx = a * dx + b * dy
        gsy = b * dx + c * dy
        grad_geo = stack_rows(
            [
                cam[0, 0] * gsx + cam[1, 0] * gsy,
                cam[0, 1] * gsx + cam[1, 1] * gsy,
                cam[0, 2] * gsx + cam[1, 2] * gsy,
                -0.5 * dxx,
                -dxy,
                -0.5 * dyy,
                one_less * m0,
            ]
        )
        for j in range(per_tile):
            lanes = slice(j * blk, (j + 1) * blk)
            val = jnp.concatenate([grad_feats[:, lanes], grad_geo[:, lanes]], axis=0)
            mine = t * per_tile + j
            held = seen[slots[j]]
            at = jnp.where(held < 0, mine, held)
            seen[slots[j]] = at
            acc[at] = jnp.where(at == mine, val, acc[at] + val)

    def some_tiles(i, carry):
        waiting = [one_tile(i * ABREAST + n, n % SLOTS) for n in range(ABREAST)]
        runs = []
        while waiting or runs:
            runs += waiting[:1]
            del waiting[:1]
            for _ in range(2):
                runs = [run for run in runs if next(run, run) is None]
        return carry

    lax.fori_loop(0, tiles // ABREAST, some_tiles, 0)

    def give(t, carry):
        for j in range(per_tile):
            s = lax.div(ids[j, t], blocks_dev)
            out[s] = acc[seen[s]].astype(bf16)
        return carry

    lax.fori_loop(0, tiles, give, 0)


def shifts(views):
    return [0] + sorted(range(1, views), key=lambda d: -min(d, views - d))


def owner_kernel(req, got, own, *rest):
    sends, acc = rest[:-1], rest[-1]
    views = len(sends) + 1
    blocks, out_rows, _ = own.shape
    share = out_rows - GEO
    acc[...] = jnp.zeros_like(acc)

    def step(i, carry):
        at = req[0, 0, i]

        @pl.when(at >= 0)
        def _():
            acc[at] = acc[at] + got[i].astype(jnp.float32)

        return carry

    lax.fori_loop(0, got.shape[0], step, 0, unroll=4)

    def lay(i, carry):
        geo = acc[i, views * share :]
        for d, ref in zip(shifts(views), (own,) + sends):
            start = pl.multiple_of(lax.rem(req[1, 0, 0] + d, views) * share, share)
            rows = jnp.concatenate([acc[i, pl.ds(start, share)], geo], axis=0)
            ref[i] = rows.astype(ref.dtype)
        return carry

    lax.fori_loop(0, blocks, lay, 0, unroll=2)


def view_kernel(own, *rest):
    got, (out_feats, out_means, out_conics, out_opac) = rest[:-4], rest[-4:]
    share = out_feats.shape[1]
    total = own[...]
    for ref in got:
        total = total + ref[...].astype(jnp.float32)
    out_feats[...] = total[:, :share]
    geo = total[:, share:]
    for k in range(3):
        out_means[k] = geo[:, k]
        out_conics[k] = geo[:, 3 + k]
    out_opac[...] = geo[:, 6]


def run_tiles(ids, cam, fetched, masks, cots, blocks_dev):
    n_scene, _, blk = fetched.shape
    tiles, channels, pixels = cots.shape
    entries = tiles * ids.shape[0]
    rows = ids.shape[0] * blk
    f32, bf16 = jnp.float32, jnp.bfloat16
    return call(
        lambda *refs: tile_kernel(blocks_dev, *refs),
        [jax.ShapeDtypeStruct((n_scene, channels + GEO, blk), bf16)],
        2, 3,
        scratch=[
            pltpu.VMEM((entries, channels + GEO, blk), f32),
            pltpu.VMEM((SLOTS, pixels, rows), f32),
            pltpu.VMEM((SLOTS, pixels, rows), f32),
            pltpu.VMEM((SLOTS, pixels, rows), bf16),
            pltpu.VMEM((SLOTS, pixels, rows), bf16),
            pltpu.VMEM((SLOTS, pixels, rows), bf16),
            pltpu.VMEM((rows, rows // 2), bf16),
            pltpu.VMEM((rows, rows // 2), bf16),
            pltpu.VMEM((pixels, 4 * GEO), bf16),
            pltpu.VMEM((2 * GEO, pixels), bf16),
            pltpu.SMEM((n_scene,), jnp.int32),
        ],
        name="tiles",
        mib=24,
    )(ids, cam, fetched, masks, cots)[0]


def body(features, means, conics, opacity, camera, lists, masks, cotangent):
    n_scene = lax.axis_size("scene")
    n_view = lax.axis_size("view")
    blocks_dev, channels, blk = features.shape
    f32, bf16, i32 = jnp.float32, jnp.bfloat16, jnp.int32
    cam = camera[0]
    ids = lists[0].T

    want = pl.pallas_call(
        lambda *refs: want_kernel(blocks_dev, *refs),
        out_shape=jax.ShapeDtypeStruct((n_scene, 1, n_scene), i32),
        in_specs=[pl.BlockSpec(memory_space=pltpu.MemorySpace.HBM)],
        out_specs=pl.BlockSpec(memory_space=VMEM),
        scratch_shapes=[pltpu.SMEM(ids.shape, i32), pltpu.SemaphoreType.DMA],
        name="want",
    )(ids)
    asked = lax.all_to_all(want, "scene", split_axis=0, concat_axis=0, tiled=True)
    width = channels + 2 * GEO
    (table,) = call(
        table_kernel, [jax.ShapeDtypeStruct((blocks_dev, width, blk), bf16)], 1, 4, name="table"
    )(cam, features, means.transpose(1, 0, 2), conics.transpose(1, 0, 2), opacity)
    answers, req = call(
        answer_kernel,
        [
            jax.ShapeDtypeStruct((n_scene, width, blk), bf16),
            jax.ShapeDtypeStruct((2, 1, n_scene), i32),
        ],
        1, 2,
        scratch=[pltpu.SMEM((1, n_scene), i32), pltpu.SemaphoreType.DMA],
        name="answer",
    )(lax.axis_index("view").reshape(1), asked, table)
    fetched = lax.all_to_all(answers, "scene", split_axis=0, concat_axis=0, tiled=True)
    grads_out = run_tiles(ids, cam, fetched, masks[0], cotangent[0], blocks_dev)
    grads_in = lax.all_to_all(grads_out, "scene", split_axis=0, concat_axis=0, tiled=True)

    share = channels // n_view
    piece = (blocks_dev, share + GEO, blk)
    own, *sends = call(
        owner_kernel,
        [jax.ShapeDtypeStruct(piece, f32)]
        + [jax.ShapeDtypeStruct(piece, bf16)] * (n_view - 1),
        1, 1,
        scratch=[pltpu.VMEM((blocks_dev, channels + GEO, blk), f32)],
        name="owner",
    )(req, grads_in)
    got = [
        lax.ppermute(send, "view", [(v, (v + d) % n_view) for v in range(n_view)])
        for d, send in zip(shifts(n_view)[1:], sends)
    ]
    grad_feats, grad_means, grad_conics, grad_opac = call(
        view_kernel,
        [
            jax.ShapeDtypeStruct((blocks_dev, share, blk), f32),
            jax.ShapeDtypeStruct((3, blocks_dev, blk), f32),
            jax.ShapeDtypeStruct((3, blocks_dev, blk), f32),
            jax.ShapeDtypeStruct((blocks_dev, blk), f32),
        ],
        0, n_view, name="views",
    )(own, *got)
    return grad_feats, grad_means.transpose(1, 0, 2), grad_conics.transpose(1, 0, 2), grad_opac


def solution(mesh):
    return jax.shard_map(
        body,
        mesh=mesh,
        in_specs=(
            P("scene", None, None),
            P("scene", None, None),
            P("scene", None, None),
            P("scene", None),
            P("view", None, None),
            P("view", "scene", None),
            P("view", "scene", None),
            P("view", "scene", None, None),
        ),
        out_specs=(
            P("scene", "view", None),
            P("scene", None, None),
            P("scene", None, None),
            P("scene", None),
        ),
        check_vma=False,
    )
```

```python
import math

import jax
import jax.numpy as jnp
from jax import lax
from jax.experimental import pallas as pl
from jax.experimental.pallas import tpu as pltpu
from jax.sharding import PartitionSpec as P

VMEM = pltpu.MemorySpace.VMEM
SMEM = pltpu.MemorySpace.SMEM
LOG2E = math.log2(math.e)
GEO = 8
ABREAST = 8
SLOTS = 4


def call(kernel, outs, n_smem, n_vmem, scratch=(), name=None, mib=8):
    return pl.pallas_call(
        kernel,
        out_shape=outs,
        in_specs=[pl.BlockSpec(memory_space=SMEM)] * n_smem
        + [pl.BlockSpec(memory_space=VMEM)] * n_vmem,
        out_specs=[pl.BlockSpec(memory_space=VMEM)] * len(outs),
        scratch_shapes=scratch,
        compiler_params=pltpu.CompilerParams(vmem_limit_bytes=mib * 1024 * 1024),
        name=name,
    )


def want_kernel(blocks_dev, lists, want, ids, sem):
    copy = pltpu.make_async_copy(lists, ids, sem)
    copy.start()
    want[...] = jnp.full(want.shape, -1, jnp.int32)
    copy.wait()
    for j in range(ids.shape[0]):
        for t in range(ids.shape[1]):
            owner = lax.div(ids[j, t], blocks_dev)
            want[owner] = jnp.full((1, want.shape[2]), ids[j, t] - owner * blocks_dev, jnp.int32)


def stack_rows(rows):
    n = rows[0].shape[1]
    row_id = lax.broadcasted_iota(jnp.int32, (GEO, n), 0)
    out = jnp.zeros((GEO, n), jnp.float32)
    for i, row in enumerate(rows):
        out = jnp.where(row_id == i, jnp.broadcast_to(row, (GEO, n)), out)
    return out


def table_kernel(cam, feats, means, conics, opac, table):
    bf16, f32 = jnp.bfloat16, jnp.float32

    def step(i, carry):
        at = pl.ds(i, 1)
        m = [means[k, at, :] for k in range(3)]
        screen = [
            cam[k, 0] * m[0] + cam[k, 1] * m[1] + cam[k, 2] * m[2] + cam[k, 3] for k in (0, 1)
        ]
        full = stack_rows(screen + [conics[k, at, :] for k in range(3)] + [opac[at, :]])
        hi = full.astype(bf16).astype(f32)
        rest = full - hi
        mid = rest.astype(bf16).astype(f32)
        low = rest - mid
        first = stack_rows([hi[k : k + 1] for k in range(6)] + [low[2:3], low[3:4]])
        second = stack_rows([mid[k : k + 1] for k in range(6)] + [low[4:5]])
        geo = jnp.concatenate([first, second], axis=0).astype(bf16)
        table[i] = jnp.concatenate([feats[i], geo], axis=0)
        return carry

    lax.fori_loop(0, feats.shape[0], step, 0, unroll=4)


def answer_kernel(asked, table, out, req, req_smem, sem):
    n = asked.shape[0]
    lane = lax.broadcasted_iota(jnp.int32, (1, n), 1)
    line = jnp.full((1, n), -1, jnp.int32)
    for i in range(n):
        line = jnp.where(lane == i, asked[i], line)
    req[...] = line
    copy = pltpu.make_async_copy(req, req_smem, sem)
    copy.start()
    copy.wait()

    def step(i, carry):
        out[i] = table[jnp.maximum(req_smem[0, i], 0)]
        return carry

    lax.fori_loop(0, n, step, 0, unroll=8)


def tile_kernel(
    blocks_dev, ids, cam, fetched, masks, cots, out,
    acc, abuf, ebuf, keeps, weights, flows, prefix, suffix, quad, quad_t, seen,
):
    tiles, channels, pixels = cots.shape
    side = math.isqrt(pixels)
    per_tile = ids.shape[0]
    n_scene, _, blk = fetched.shape
    rows = per_tile * blk
    half = rows // 2
    f32, bf16 = jnp.float32, jnp.bfloat16

    def dot(a, b):
        return jnp.dot(a, b, preferred_element_type=f32)

    ki = lax.broadcasted_iota(jnp.int32, (half, half), 0)
    ri = lax.broadcasted_iota(jnp.int32, (half, half), 1)
    one = jnp.ones((half, half), bf16)
    up = jnp.where(ki < ri, 1.0, 0.0).astype(bf16)
    prefix[:half] = one
    prefix[half:] = up
    suffix[:half] = jnp.where(ki > ri, 1.0, 0.0).astype(bf16)
    suffix[half:] = one

    def monomials(shape, pix_dim):
        pix = lax.broadcasted_iota(jnp.int32, shape, pix_dim)
        col = lax.broadcasted_iota(jnp.int32, shape, 1 - pix_dim) % GEO
        u = (pix % side).astype(f32) - 0.5 * (side - 1)
        w = (pix // side).astype(f32) - 0.5 * (side - 1)
        val = jnp.where(col == 0, 1.0, 0.0)
        for i, m in enumerate((u, w, u * u, u * w, w * w)):
            val = jnp.where(col == i + 1, m, val)
        return val.astype(bf16)

    quad[...] = monomials(quad.shape, 0)
    quad_t[...] = monomials(quad_t.shape, 1)

    def clear(i, carry):
        seen[i] = -1
        return carry

    lax.fori_loop(0, n_scene, clear, 0, unroll=8)

    def one_tile(t, n):
        slots = [lax.div(ids[j, t], blocks_dev) for j in range(per_tile)]
        parts = jnp.concatenate([fetched[s, channels:] for s in slots], axis=1).astype(f32)
        g = parts[:GEO] + parts[GEO:]
        sx, sy, op = g[0:1], g[1:2], g[5:6]
        a = g[2:3] + parts[6:7]
        b = g[3:4] + parts[7:8]
        c = g[4:5] + parts[14:15]
        live = masks[pl.ds(t, 1), :]
        ax_by = a * sx + b * sy
        bx_cy = b * sx + c * sy
        neg = jnp.exp(-op)
        log_sig = -jnp.log(1.0 + neg)
        one_less = neg / (1.0 + neg)
        const = log_sig - 0.5 * (sx * ax_by + sy * bx_cy)
        const = jnp.where(live > 0, const * LOG2E, -1e30)
        coef = stack_rows(
            [
                const,
                ax_by * LOG2E,
                bx_cy * LOG2E,
                a * (-0.5 * LOG2E),
                b * (-LOG2E),
                c * (-0.5 * LOG2E),
            ]
        )
        hi = coef.astype(bf16).astype(f32)
        rest = coef - hi
        mid = rest.astype(bf16).astype(f32)
        coefs = jnp.concatenate([hi, mid, rest - mid, jnp.zeros_like(hi)], axis=0).astype(bf16)

        for q in (0, 1):
            cols = slice(q * half, (q + 1) * half)
            yield
            power = dot(quad[...], coefs[:, cols])
            alpha = jnp.exp2(power)
            abuf[n, :, cols] = alpha
            keep = jnp.log(1.0 - alpha) * LOG2E
            keeps[n, :, cols] = keep.astype(bf16)
            ebuf[n, :, cols] = jnp.exp2(power - keep)

        cot = cots[t]
        feat_rows = jnp.concatenate([fetched[s, :channels] for s in slots], axis=1)
        for q in (0, 1):
            cols = slice(q * half, (q + 1) * half)
            yield
            if q:
                before = dot(keeps[n], prefix[...])
            else:
                before = dot(keeps[n, :, :half], prefix[half:])
            weight = jnp.exp2(before) * abuf[n, :, cols]
            weights[n, :, cols] = weight.astype(bf16)
            flow = weight * lax.dot_general(
                cot, feat_rows[:, cols], (((0,), (0,)), ((), ())), preferred_element_type=f32
            )
            abuf[n, :, cols] = flow
            flows[n, :, cols] = flow.astype(bf16)
        yield
        grad_feats = dot(cot, weights[n])
        for q in (0, 1):
            cols = slice(q * half, (q + 1) * half)
            yield
            if q:
                behind = dot(flows[n, :, half:], suffix[:half])
            else:
                behind = dot(flows[n], suffix[...])
            weights[n, :, cols] = (abuf[n, :, cols] - ebuf[n, :, cols] * behind).astype(bf16)
        yield
        mom = dot(quad_t[...], weights[n])
        m0, mu, mw, muu, muw, mww = [mom[i : i + 1] for i in range(6)]
        dx = mu - sx * m0
        dy = mw - sy * m0
        dxx = muu - sx * (mu + dx)
        dxy = muw - sx * mw - sy * dx
        dyy = mww - sy * (mw + dy)
        gsx = a * dx + b * dy
        gsy = b * dx + c * dy
        grad_geo = stack_rows(
            [
                cam[0, 0] * gsx + cam[1, 0] * gsy,
                cam[0, 1] * gsx + cam[1, 1] * gsy,
                cam[0, 2] * gsx + cam[1, 2] * gsy,
                -0.5 * dxx,
                -dxy,
                -0.5 * dyy,
                one_less * m0,
            ]
        )
        for j in range(per_tile):
            lanes = slice(j * blk, (j + 1) * blk)
            val = jnp.concatenate([grad_feats[:, lanes], grad_geo[:, lanes]], axis=0)
            mine = t * per_tile + j
            held = seen[slots[j]]
            at = jnp.where(held < 0, mine, held)
            seen[slots[j]] = at
            acc[at] = jnp.where(at == mine, val, acc[at] + val)

    def some_tiles(i, carry):
        waiting = [one_tile(i * ABREAST + n, n % SLOTS) for n in range(ABREAST)]
        runs = []
        while waiting or runs:
            runs += waiting[:1]
            del waiting[:1]
            for _ in range(2):
                runs = [run for run in runs if next(run, run) is None]
        return carry

    lax.fori_loop(0, tiles // ABREAST, some_tiles, 0)

    def give(t, carry):
        for j in range(per_tile):
            s = lax.div(ids[j, t], blocks_dev)
            out[s] = acc[seen[s]].astype(bf16)
        return carry

    lax.fori_loop(0, tiles, give, 0)


def owner_kernel(req, got, out, acc):
    views, blocks, out_rows, _ = out.shape
    share = out_rows - GEO
    acc[...] = jnp.zeros_like(acc)

    def step(i, carry):
        at = req[0, i]

        @pl.when(at >= 0)
        def _():
            acc[at] = acc[at] + got[i].astype(jnp.float32)

        return carry

    lax.fori_loop(0, got.shape[0], step, 0, unroll=16)

    def lay(i, carry):
        rows = acc[i].astype(jnp.bfloat16)
        for v in range(views):
            out[v, i] = jnp.concatenate(
                [rows[v * share : (v + 1) * share], rows[views * share :]], axis=0
            )
        return carry

    lax.fori_loop(0, blocks, lay, 0, unroll=4)


def view_kernel(got, out_feats, out_means, out_conics, out_opac):
    share = out_feats.shape[1]
    total = got[0].astype(jnp.float32)
    for v in range(1, got.shape[0]):
        total = total + got[v].astype(jnp.float32)
    out_feats[...] = total[:, :share]
    geo = total[:, share:]
    for k in range(3):
        out_means[k] = geo[:, k]
        out_conics[k] = geo[:, 3 + k]
    out_opac[...] = geo[:, 6]


def run_tiles(ids, cam, fetched, masks, cots, blocks_dev):
    n_scene, _, blk = fetched.shape
    tiles, channels, pixels = cots.shape
    entries = tiles * ids.shape[0]
    rows = ids.shape[0] * blk
    f32, bf16 = jnp.float32, jnp.bfloat16
    return call(
        lambda *refs: tile_kernel(blocks_dev, *refs),
        [jax.ShapeDtypeStruct((n_scene, channels + GEO, blk), bf16)],
        2, 3,
        scratch=[
            pltpu.VMEM((entries, channels + GEO, blk), f32),
            pltpu.VMEM((SLOTS, pixels, rows), f32),
            pltpu.VMEM((SLOTS, pixels, rows), f32),
            pltpu.VMEM((SLOTS, pixels, rows), bf16),
            pltpu.VMEM((SLOTS, pixels, rows), bf16),
            pltpu.VMEM((SLOTS, pixels, rows), bf16),
            pltpu.VMEM((rows, rows // 2), bf16),
            pltpu.VMEM((rows, rows // 2), bf16),
            pltpu.VMEM((pixels, 4 * GEO), bf16),
            pltpu.VMEM((2 * GEO, pixels), bf16),
            pltpu.SMEM((n_scene,), jnp.int32),
        ],
        name="tiles",
        mib=24,
    )(ids, cam, fetched, masks, cots)[0]


def body(features, means, conics, opacity, camera, lists, masks, cotangent):
    n_scene = lax.axis_size("scene")
    n_view = lax.axis_size("view")
    blocks_dev, channels, blk = features.shape
    f32, bf16, i32 = jnp.float32, jnp.bfloat16, jnp.int32
    cam = camera[0]
    ids = lists[0].T

    want = pl.pallas_call(
        lambda *refs: want_kernel(blocks_dev, *refs),
        out_shape=jax.ShapeDtypeStruct((n_scene, 1, n_scene), i32),
        in_specs=[pl.BlockSpec(memory_space=pltpu.MemorySpace.HBM)],
        out_specs=pl.BlockSpec(memory_space=VMEM),
        scratch_shapes=[pltpu.SMEM(ids.shape, i32), pltpu.SemaphoreType.DMA],
        name="want",
    )(ids)
    asked = lax.all_to_all(want, "scene", split_axis=0, concat_axis=0, tiled=True)
    width = channels + 2 * GEO
    (table,) = call(
        table_kernel, [jax.ShapeDtypeStruct((blocks_dev, width, blk), bf16)], 1, 4, name="table"
    )(cam, features, means.transpose(1, 0, 2), conics.transpose(1, 0, 2), opacity)
    answers, req = call(
        answer_kernel,
        [
            jax.ShapeDtypeStruct((n_scene, width, blk), bf16),
            jax.ShapeDtypeStruct((1, n_scene), i32),
        ],
        0, 2,
        scratch=[pltpu.SMEM((1, n_scene), i32), pltpu.SemaphoreType.DMA],
        name="answer",
    )(asked, table)
    fetched = lax.all_to_all(answers, "scene", split_axis=0, concat_axis=0, tiled=True)
    grads_out = run_tiles(ids, cam, fetched, masks[0], cotangent[0], blocks_dev)
    grads_in = lax.all_to_all(grads_out, "scene", split_axis=0, concat_axis=0, tiled=True)

    share = channels // n_view
    (sums_out,) = call(
        owner_kernel,
        [jax.ShapeDtypeStruct((n_view, blocks_dev, share + GEO, blk), bf16)],
        1, 1,
        scratch=[pltpu.VMEM((blocks_dev, channels + GEO, blk), f32)],
        name="owner",
    )(req, grads_in)
    sums_in = lax.all_to_all(sums_out, "view", split_axis=0, concat_axis=0, tiled=True)
    grad_feats, grad_means, grad_conics, grad_opac = call(
        view_kernel,
        [
            jax.ShapeDtypeStruct((blocks_dev, share, blk), f32),
            jax.ShapeDtypeStruct((3, blocks_dev, blk), f32),
            jax.ShapeDtypeStruct((3, blocks_dev, blk), f32),
            jax.ShapeDtypeStruct((blocks_dev, blk), f32),
        ],
        0, 1, name="views",
    )(sums_in)
    return grad_feats, grad_means.transpose(1, 0, 2), grad_conics.transpose(1, 0, 2), grad_opac


def solution(mesh):
    return jax.shard_map(
        body,
        mesh=mesh,
        in_specs=(
            P("scene", None, None),
            P("scene", None, None),
            P("scene", None, None),
            P("scene", None),
            P("view", None, None),
            P("view", "scene", None),
            P("view", "scene", None),
            P("view", "scene", None, None),
        ),
        out_specs=(
            P("scene", "view", None),
            P("scene", None, None),
            P("scene", None, None),
            P("scene", None),
        ),
        check_vma=False,
    )
```

```python
import math

import jax
import jax.numpy as jnp
from jax import lax
from jax.experimental import pallas as pl
from jax.experimental.pallas import tpu as pltpu
from jax.sharding import PartitionSpec as P

VMEM = pltpu.MemorySpace.VMEM
SMEM = pltpu.MemorySpace.SMEM
LOG2E = math.log2(math.e)
GEO = 8
ABREAST = 8
SLOTS = 4


def call(kernel, outs, n_smem, n_vmem, scratch=(), name=None, mib=8):
    return pl.pallas_call(
        kernel,
        out_shape=outs,
        in_specs=[pl.BlockSpec(memory_space=SMEM)] * n_smem
        + [pl.BlockSpec(memory_space=VMEM)] * n_vmem,
        out_specs=[pl.BlockSpec(memory_space=VMEM)] * len(outs),
        scratch_shapes=scratch,
        compiler_params=pltpu.CompilerParams(vmem_limit_bytes=mib * 1024 * 1024),
        name=name,
    )


def want_kernel(blocks_dev, lists, want, ids, sem):
    copy = pltpu.make_async_copy(lists, ids, sem)
    copy.start()
    want[...] = jnp.full(want.shape, -1, jnp.int32)
    copy.wait()
    for j in range(ids.shape[0]):
        for t in range(ids.shape[1]):
            owner = lax.div(ids[j, t], blocks_dev)
            want[owner] = jnp.full((1, want.shape[2]), ids[j, t] - owner * blocks_dev, jnp.int32)


def stack_rows(rows):
    n = rows[0].shape[1]
    row_id = lax.broadcasted_iota(jnp.int32, (GEO, n), 0)
    out = jnp.zeros((GEO, n), jnp.float32)
    for i, row in enumerate(rows):
        out = jnp.where(row_id == i, jnp.broadcast_to(row, (GEO, n)), out)
    return out


def table_kernel(cam, feats, means, conics, opac, table):
    bf16, f32 = jnp.bfloat16, jnp.float32

    def step(i, carry):
        at = pl.ds(i, 1)
        m = [means[k, at, :] for k in range(3)]
        screen = [
            cam[k, 0] * m[0] + cam[k, 1] * m[1] + cam[k, 2] * m[2] + cam[k, 3] for k in (0, 1)
        ]
        full = stack_rows(screen + [conics[k, at, :] for k in range(3)] + [opac[at, :]])
        hi = full.astype(bf16).astype(f32)
        rest = full - hi
        mid = rest.astype(bf16).astype(f32)
        low = rest - mid
        first = stack_rows([hi[k : k + 1] for k in range(6)] + [low[2:3], low[3:4]])
        second = stack_rows([mid[k : k + 1] for k in range(6)] + [low[4:5]])
        geo = jnp.concatenate([first, second], axis=0).astype(bf16)
        table[i] = jnp.concatenate([feats[i], geo], axis=0)
        return carry

    lax.fori_loop(0, feats.shape[0], step, 0, unroll=4)


def answer_kernel(view, asked, table, out, req, req_smem, sem):
    n = asked.shape[0]
    lane = lax.broadcasted_iota(jnp.int32, (1, n), 1)
    line = jnp.full((1, n), -1, jnp.int32)
    for i in range(n):
        line = jnp.where(lane == i, asked[i], line)
    req[0] = line
    req[1] = jnp.full((1, n), view[0], jnp.int32)
    copy = pltpu.make_async_copy(req.at[0], req_smem, sem)
    copy.start()
    copy.wait()

    def step(i, carry):
        out[i] = table[jnp.maximum(req_smem[0, i], 0)]
        return carry

    lax.fori_loop(0, n, step, 0, unroll=8)


def tile_kernel(
    blocks_dev, ids, cam, fetched, masks, cots, out,
    acc, abuf, ebuf, keeps, weights, flows, prefix, suffix, quad, quad_t, seen,
):
    tiles, channels, pixels = cots.shape
    side = math.isqrt(pixels)
    per_tile = ids.shape[0]
    n_scene, _, blk = fetched.shape
    rows = per_tile * blk
    half = rows // 2
    f32, bf16 = jnp.float32, jnp.bfloat16

    def dot(a, b):
        return jnp.dot(a, b, preferred_element_type=f32)

    ki = lax.broadcasted_iota(jnp.int32, (half, half), 0)
    ri = lax.broadcasted_iota(jnp.int32, (half, half), 1)
    one = jnp.ones((half, half), bf16)
    up = jnp.where(ki < ri, 1.0, 0.0).astype(bf16)
    prefix[:half] = one
    prefix[half:] = up
    suffix[:half] = jnp.where(ki > ri, 1.0, 0.0).astype(bf16)
    suffix[half:] = one

    def monomials(shape, pix_dim):
        pix = lax.broadcasted_iota(jnp.int32, shape, pix_dim)
        col = lax.broadcasted_iota(jnp.int32, shape, 1 - pix_dim) % GEO
        u = (pix % side).astype(f32) - 0.5 * (side - 1)
        w = (pix // side).astype(f32) - 0.5 * (side - 1)
        val = jnp.where(col == 0, 1.0, 0.0)
        for i, m in enumerate((u, w, u * u, u * w, w * w)):
            val = jnp.where(col == i + 1, m, val)
        return val.astype(bf16)

    quad[...] = monomials(quad.shape, 0)
    quad_t[...] = monomials(quad_t.shape, 1)

    def clear(i, carry):
        seen[i] = -1
        return carry

    lax.fori_loop(0, n_scene, clear, 0, unroll=8)

    def one_tile(t, n):
        slots = [lax.div(ids[j, t], blocks_dev) for j in range(per_tile)]
        parts = jnp.concatenate([fetched[s, channels:] for s in slots], axis=1).astype(f32)
        g = parts[:GEO] + parts[GEO:]
        sx, sy, op = g[0:1], g[1:2], g[5:6]
        a = g[2:3] + parts[6:7]
        b = g[3:4] + parts[7:8]
        c = g[4:5] + parts[14:15]
        live = masks[pl.ds(t, 1), :]
        ax_by = a * sx + b * sy
        bx_cy = b * sx + c * sy
        neg = jnp.exp(-op)
        log_sig = -jnp.log(1.0 + neg)
        one_less = neg / (1.0 + neg)
        const = log_sig - 0.5 * (sx * ax_by + sy * bx_cy)
        const = jnp.where(live > 0, const * LOG2E, -1e30)
        coef = stack_rows(
            [
                const,
                ax_by * LOG2E,
                bx_cy * LOG2E,
                a * (-0.5 * LOG2E),
                b * (-LOG2E),
                c * (-0.5 * LOG2E),
            ]
        )
        hi = coef.astype(bf16).astype(f32)
        rest = coef - hi
        mid = rest.astype(bf16).astype(f32)
        coefs = jnp.concatenate([hi, mid, rest - mid, jnp.zeros_like(hi)], axis=0).astype(bf16)

        for q in (0, 1):
            cols = slice(q * half, (q + 1) * half)
            yield
            power = dot(quad[...], coefs[:, cols])
            alpha = jnp.exp2(power)
            abuf[n, :, cols] = alpha
            keep = jnp.log(1.0 - alpha) * LOG2E
            keeps[n, :, cols] = keep.astype(bf16)
            ebuf[n, :, cols] = jnp.exp2(power - keep)

        cot = cots[t]
        feat_rows = jnp.concatenate([fetched[s, :channels] for s in slots], axis=1)
        for q in (0, 1):
            cols = slice(q * half, (q + 1) * half)
            yield
            if q:
                before = dot(keeps[n], prefix[...])
            else:
                before = dot(keeps[n, :, :half], prefix[half:])
            weight = jnp.exp2(before) * abuf[n, :, cols]
            weights[n, :, cols] = weight.astype(bf16)
            flow = weight * lax.dot_general(
                cot, feat_rows[:, cols], (((0,), (0,)), ((), ())), preferred_element_type=f32
            )
            abuf[n, :, cols] = flow
            flows[n, :, cols] = flow.astype(bf16)
        yield
        grad_feats = dot(cot, weights[n])
        for q in (0, 1):
            cols = slice(q * half, (q + 1) * half)
            yield
            if q:
                behind = dot(flows[n, :, half:], suffix[:half])
            else:
                behind = dot(flows[n], suffix[...])
            weights[n, :, cols] = (abuf[n, :, cols] - ebuf[n, :, cols] * behind).astype(bf16)
        yield
        mom = dot(quad_t[...], weights[n])
        m0, mu, mw, muu, muw, mww = [mom[i : i + 1] for i in range(6)]
        dx = mu - sx * m0
        dy = mw - sy * m0
        dxx = muu - sx * (mu + dx)
        dxy = muw - sx * mw - sy * dx
        dyy = mww - sy * (mw + dy)
        gsx = a * dx + b * dy
        gsy = b * dx + c * dy
        grad_geo = stack_rows(
            [
                cam[0, 0] * gsx + cam[1, 0] * gsy,
                cam[0, 1] * gsx + cam[1, 1] * gsy,
                cam[0, 2] * gsx + cam[1, 2] * gsy,
                -0.5 * dxx,
                -dxy,
                -0.5 * dyy,
                one_less * m0,
            ]
        )
        for j in range(per_tile):
            lanes = slice(j * blk, (j + 1) * blk)
            val = jnp.concatenate([grad_feats[:, lanes], grad_geo[:, lanes]], axis=0)
            mine = t * per_tile + j
            held = seen[slots[j]]
            at = jnp.where(held < 0, mine, held)
            seen[slots[j]] = at
            acc[at] = jnp.where(at == mine, val, acc[at] + val)

    def some_tiles(i, carry):
        waiting = [one_tile(i * ABREAST + n, n % SLOTS) for n in range(ABREAST)]
        runs = []
        while waiting or runs:
            runs += waiting[:1]
            del waiting[:1]
            for _ in range(2):
                runs = [run for run in runs if next(run, run) is None]
        return carry

    lax.fori_loop(0, tiles // ABREAST, some_tiles, 0)

    def give(t, carry):
        for j in range(per_tile):
            s = lax.div(ids[j, t], blocks_dev)
            out[s] = acc[seen[s]].astype(bf16)
        return carry

    lax.fori_loop(0, tiles, give, 0)


def shifts(views):
    return [0] + sorted(range(1, views), key=lambda d: -min(d, views - d))


def owner_kernel(req, got, own, *rest):
    sends, acc = rest[:-1], rest[-1]
    views = len(sends) + 1
    blocks, out_rows, _ = own.shape
    share = out_rows - GEO
    acc[...] = jnp.zeros_like(acc)

    def step(i, carry):
        at = req[0, 0, i]

        @pl.when(at >= 0)
        def _():
            acc[at] = acc[at] + got[i].astype(jnp.float32)

        return carry

    lax.fori_loop(0, got.shape[0], step, 0, unroll=16)

    def lay(i, carry):
        geo = acc[i, views * share :]
        for d, ref in zip(shifts(views), (own,) + sends):
            start = pl.multiple_of(lax.rem(req[1, 0, 0] + d, views) * share, share)
            rows = jnp.concatenate([acc[i, pl.ds(start, share)], geo], axis=0)
            ref[i] = rows.astype(ref.dtype)
        return carry

    lax.fori_loop(0, blocks, lay, 0, unroll=4)


def view_kernel(own, *rest):
    got, (out_feats, out_means, out_conics, out_opac) = rest[:-4], rest[-4:]
    share = out_feats.shape[1]
    total = own[...]
    for ref in got:
        total = total + ref[...].astype(jnp.float32)
    out_feats[...] = total[:, :share]
    geo = total[:, share:]
    for k in range(3):
        out_means[k] = geo[:, k]
        out_conics[k] = geo[:, 3 + k]
    out_opac[...] = geo[:, 6]


def run_tiles(ids, cam, fetched, masks, cots, blocks_dev):
    n_scene, _, blk = fetched.shape
    tiles, channels, pixels = cots.shape
    entries = tiles * ids.shape[0]
    rows = ids.shape[0] * blk
    f32, bf16 = jnp.float32, jnp.bfloat16
    return call(
        lambda *refs: tile_kernel(blocks_dev, *refs),
        [jax.ShapeDtypeStruct((n_scene, channels + GEO, blk), bf16)],
        2, 3,
        scratch=[
            pltpu.VMEM((entries, channels + GEO, blk), f32),
            pltpu.VMEM((SLOTS, pixels, rows), f32),
            pltpu.VMEM((SLOTS, pixels, rows), f32),
            pltpu.VMEM((SLOTS, pixels, rows), bf16),
            pltpu.VMEM((SLOTS, pixels, rows), bf16),
            pltpu.VMEM((SLOTS, pixels, rows), bf16),
            pltpu.VMEM((rows, rows // 2), bf16),
            pltpu.VMEM((rows, rows // 2), bf16),
            pltpu.VMEM((pixels, 4 * GEO), bf16),
            pltpu.VMEM((2 * GEO, pixels), bf16),
            pltpu.SMEM((n_scene,), jnp.int32),
        ],
        name="tiles",
        mib=24,
    )(ids, cam, fetched, masks, cots)[0]


def body(features, means, conics, opacity, camera, lists, masks, cotangent):
    n_scene = lax.axis_size("scene")
    n_view = lax.axis_size("view")
    blocks_dev, channels, blk = features.shape
    f32, bf16, i32 = jnp.float32, jnp.bfloat16, jnp.int32
    cam = camera[0]
    ids = lists[0].T

    want = pl.pallas_call(
        lambda *refs: want_kernel(blocks_dev, *refs),
        out_shape=jax.ShapeDtypeStruct((n_scene, 1, n_scene), i32),
        in_specs=[pl.BlockSpec(memory_space=pltpu.MemorySpace.HBM)],
        out_specs=pl.BlockSpec(memory_space=VMEM),
        scratch_shapes=[pltpu.SMEM(ids.shape, i32), pltpu.SemaphoreType.DMA],
        name="want",
    )(ids)
    asked = lax.all_to_all(want, "scene", split_axis=0, concat_axis=0, tiled=True)
    width = channels + 2 * GEO
    (table,) = call(
        table_kernel, [jax.ShapeDtypeStruct((blocks_dev, width, blk), bf16)], 1, 4, name="table"
    )(cam, features, means.transpose(1, 0, 2), conics.transpose(1, 0, 2), opacity)
    answers, req = call(
        answer_kernel,
        [
            jax.ShapeDtypeStruct((n_scene, width, blk), bf16),
            jax.ShapeDtypeStruct((2, 1, n_scene), i32),
        ],
        1, 2,
        scratch=[pltpu.SMEM((1, n_scene), i32), pltpu.SemaphoreType.DMA],
        name="answer",
    )(lax.axis_index("view").reshape(1), asked, table)
    fetched = lax.all_to_all(answers, "scene", split_axis=0, concat_axis=0, tiled=True)
    grads_out = run_tiles(ids, cam, fetched, masks[0], cotangent[0], blocks_dev)
    grads_in = lax.all_to_all(grads_out, "scene", split_axis=0, concat_axis=0, tiled=True)

    share = channels // n_view
    piece = (blocks_dev, share + GEO, blk)
    own, *sends = call(
        owner_kernel,
        [jax.ShapeDtypeStruct(piece, f32)]
        + [jax.ShapeDtypeStruct(piece, bf16)] * (n_view - 1),
        1, 1,
        scratch=[pltpu.VMEM((blocks_dev, channels + GEO, blk), f32)],
        name="owner",
    )(req, grads_in)
    got = [
        lax.ppermute(send, "view", [(v, (v + d) % n_view) for v in range(n_view)])
        for d, send in zip(shifts(n_view)[1:], sends)
    ]
    grad_feats, grad_means, grad_conics, grad_opac = call(
        view_kernel,
        [
            jax.ShapeDtypeStruct((blocks_dev, share, blk), f32),
            jax.ShapeDtypeStruct((3, blocks_dev, blk), f32),
            jax.ShapeDtypeStruct((3, blocks_dev, blk), f32),
            jax.ShapeDtypeStruct((blocks_dev, blk), f32),
        ],
        0, n_view, name="views",
    )(own, *got)
    return grad_feats, grad_means.transpose(1, 0, 2), grad_conics.transpose(1, 0, 2), grad_opac


def solution(mesh):
    return jax.shard_map(
        body,
        mesh=mesh,
        in_specs=(
            P("scene", None, None),
            P("scene", None, None),
            P("scene", None, None),
            P("scene", None),
            P("view", None, None),
            P("view", "scene", None),
            P("view", "scene", None),
            P("view", "scene", None, None),
        ),
        out_specs=(
            P("scene", "view", None),
            P("scene", None, None),
            P("scene", None, None),
            P("scene", None),
        ),
        check_vma=False,
    )
```
